256 devices in a mesh: gz: 64 (over z, x, y_hi), gx: 2 (over core), gy: 2 (over y_lo).
Axes of the slice: x: 4, y: 4 (y_hi: 2, y_lo: 2; y = y_hi * 2 + y_lo), z: 8, core: 2. Of those that a mesh axis runs over, the one named last changes fastest.
Arguments:
- rhs_field: float32 [128, 8, 8, 512], P('gz', 'gy', 'gx'), may hold values from -1 to 1
- start_field: float32 [128, 8, 8, 512], P('gz', 'gy', 'gx'), may hold values from -0.2 to 0.2
- material: int32 [128, 8, 8], P('gz', 'gy', 'gx'), may hold values from 0 to 3
- diag_inverse: float32 [4, 64, 64], replicated, may hold values from -0.2 to 0.2
- z_blocks: float32 [4, 2, 64, 64], replicated, may hold values from -10 to 10
- side_blocks: float32 [4, 4, 64, 64], replicated, may hold values from -0.375 to 0.375
Outputs:
- forward_field: float32 [128, 8, 8, 512], P('gz', 'gy', 'gx')
- backward_field: float32 [128, 8, 8, 512], P('gz', 'gy', 'gx')
The draws below stay inside these ranges and needn't reach their ends.
Inputs may be any that keep to these rules, and one draw needn't show every extreme that they name: material[e] selects the element's tables.
All inputs are finite; a program needn't handle non-finite values.
Results may differ from the reference program's by a relative error of at most 0.0003.
Values sent between devices are 32-bit elements; how exact they have to be, the bound alone decides.
No kernel may reach another device: no remote copies, remote signals or barrier semaphores. Data moves between devices by JAX's collectives and lax.ppermute only.
A program may use at most 128 MiB of HBM per device.

```python
import jax
import jax.numpy as jnp
from jax import lax

DOFS = 64
RHS = 8
MATS = 4
NX = 8
NY = 8
NZ = 128


HIGH = lax.Precision.HIGHEST


def reflections(base_key, order):
    vectors = jax.random.normal(base_key, (order, order), jnp.float32)

    def reflect(position, current):
        direction = vectors[position]
        image = jnp.dot(current, direction, precision=HIGH)
        return current - 2.0 / jnp.sum(direction * direction) * image[:, None] * direction[None, :]
    return lax.fori_loop(0, order, reflect, jnp.eye(order, dtype=jnp.float32))


def shared_tables(base_key):
    root = jax.random.fold_in(base_key, 7321)
    scale_low, scale_high, keep_low, keep_high = (0.1, 0.2, 0.995, 0.999)
    inverses = []
    couplings = []
    for which_kind in range(MATS):
        kind_key = jax.random.fold_in(root, which_kind)
        rotation = reflections(jax.random.fold_in(kind_key, 11), DOFS)
        factor = jax.random.uniform(jax.random.fold_in(kind_key, 13), (), jnp.float32, scale_low, scale_high)
        inverses.append(factor * rotation)
        pair = []
        for which_side in range(2):
            side_key = jax.random.fold_in(kind_key, 17 + which_side)
            turning = reflections(jax.random.fold_in(side_key, 19), DOFS)
            keeping = jax.random.uniform(jax.random.fold_in(side_key, 23), (), jnp.float32, keep_low, keep_high)
            coupled = jnp.dot(turning, rotation.T, precision=HIGH)
            pair.append(-(keeping / factor) * coupled)
        couplings.append(jnp.stack(pair, axis=0))
    return (jnp.stack(inverses, axis=0), jnp.stack(couplings, axis=0))


def draw_diag_inverse(key, part):
    inverses, couplings = shared_tables(key)
    return inverses.astype(jnp.float32)


def draw_z_blocks(key, part):
    inverses, couplings = shared_tables(key)
    return couplings.astype(jnp.float32)


def set_ends(drawn, key, smallest, top_value):
    index_at = [jax.random.randint(jax.random.fold_in(key, axis), (), 0, length) for axis, length in enumerate(drawn.shape)]
    widest = drawn.shape.index(max(drawn.shape))
    neighbour = index_at[:widest] + [(index_at[widest] + 1) % drawn.shape[widest]] + index_at[widest + 1:]
    return drawn.at[tuple(index_at)].set(smallest).at[tuple(neighbour)].set(top_value)


def shard_levels(rng, shape, cuts, least, top_value):
    def one(dim, shards_of):
        heights = jax.random.uniform(jax.random.fold_in(jax.random.fold_in(rng, 6), dim), (shards_of,), jnp.float32, least / len(cuts), top_value / len(cuts))
        return jnp.repeat(jnp.exp(heights), shape[dim] // shards_of).reshape((-1,) + (1,) * (len(shape) - dim - 1))

    level = one(*cuts[0])
    for cut in cuts[1:]:
        level = level * one(*cut)
    return level


def bell_draw(rng, shape, deviation, reach, split=(), kind=jnp.bfloat16):
    drawn = jax.random.normal(rng, shape, jnp.float32) * deviation
    if len(split) > 0:
        drawn = shard_levels(rng, shape, split, -0.22, 0.18) * drawn
    return jnp.clip(drawn, min=-reach, max=reach).astype(kind)


def setup_inputs(seed: int = 0) -> dict:
    keys = jax.random.split(jax.random.key(seed), 7)
    rhs_field = bell_draw(keys[0], (NZ, NY, NX, RHS * DOFS), 0.15, 1.0, ((0, 64), (1, 2), (2, 2)), jnp.float32)
    start_field = bell_draw(keys[1], (NZ, NY, NX, RHS * DOFS), 0.03, 0.2, ((0, 64), (1, 2), (2, 2)), jnp.float32)
    material = set_ends(jax.random.randint(keys[2], (NZ, NY, NX), 0, MATS), jax.random.fold_in(keys[2], 1), 0, MATS - 1).astype(jnp.int32)
    diag_inverse = draw_diag_inverse(jax.random.fold_in(keys[6], 71), 0)
    z_blocks = draw_z_blocks(jax.random.fold_in(keys[6], 71), 0)
    side_blocks = bell_draw(keys[5], (MATS, 4, DOFS, DOFS), (DOFS * 4) ** -0.5, 0.375, (), jnp.float32)
    return dict(rhs_field=rhs_field, start_field=start_field, material=material, diag_inverse=diag_inverse, z_blocks=z_blocks, side_blocks=side_blocks)


HIGH = lax.Precision.HIGHEST


def apply_tables(stacked, tables, selector):
    inner = stacked.shape[-1]
    kinds = tables.shape[0]
    merged = jnp.transpose(tables, (1, 0, 2)).reshape(inner, kinds * tables.shape[2])
    product = jnp.dot(stacked.reshape(-1, inner), merged, precision=HIGH, preferred_element_type=jnp.float32)
    product = product.reshape(stacked.shape[0], stacked.shape[1], kinds, tables.shape[2])
    return jnp.sum(product * selector[:, None, :, None], axis=2)


def plane_known(rhs_plane, z_plane, source_plane, selector, z_table, side_blocks):
    height, across = source_plane.shape[0], source_plane.shape[1]
    padded = jnp.pad(source_plane, ((1, 1), (1, 1), (0, 0), (0, 0)))
    pieces = [z_plane, padded[:-2, 1:-1], padded[2:, 1:-1], padded[1:-1, :-2], padded[1:-1, 2:]]
    stacked = jnp.concatenate([piece.reshape(height * across, RHS, DOFS) for piece in pieces], axis=-1)
    tables = jnp.concatenate([z_table[:, None], side_blocks], axis=1).reshape(MATS, 5 * DOFS, DOFS)
    return rhs_plane.reshape(height * across, RHS, DOFS) - apply_tables(stacked, tables, selector)


def reference(rhs_field, start_field, material, diag_inverse, z_blocks, side_blocks):
    planes, height, across, width = rhs_field.shape
    full_shape = (planes, height, across, RHS, DOFS)
    rhs_all = rhs_field.reshape(full_shape)
    start = start_field.reshape(full_shape)
    selector = (material[..., None] == jnp.arange(MATS, dtype=jnp.int32)).astype(jnp.float32)
    selector = selector.reshape(planes, height * across, MATS)
    zero_plane = jnp.zeros((1, height, across, RHS, DOFS), jnp.float32)
    upper_old = jnp.concatenate([start[1:], zero_plane], axis=0)

    def forward_step(below, inputs):
        rhs_plane, z_plane, source_plane, plane_sel = inputs
        known_part = plane_known(rhs_plane, z_plane, source_plane, plane_sel, z_blocks[:, 1], side_blocks)
        residual = known_part - apply_tables(below.reshape(height * across, RHS, DOFS), z_blocks[:, 0], plane_sel)
        solved = apply_tables(residual, diag_inverse, plane_sel).reshape(height, across, RHS, DOFS)
        return solved, solved

    unused, forward = lax.scan(forward_step, zero_plane[0], (rhs_all, upper_old, start, selector))
    lower_new = jnp.concatenate([zero_plane, forward[:-1]], axis=0)

    def backward_step(above, inputs):
        rhs_plane, z_plane, source_plane, plane_sel = inputs
        known_part = plane_known(rhs_plane, z_plane, source_plane, plane_sel, z_blocks[:, 0], side_blocks)
        residual = known_part - apply_tables(above.reshape(height * across, RHS, DOFS), z_blocks[:, 1], plane_sel)
        solved = apply_tables(residual, diag_inverse, plane_sel).reshape(height, across, RHS, DOFS)
        return solved, solved

    unused_two, backward = lax.scan(backward_step, zero_plane[0], (rhs_all, lower_new, forward, selector), reverse=True)
    return forward.reshape(planes, height, across, width), backward.reshape(planes, height, across, width)
```

```python
import functools

import jax
import jax.numpy as jnp
from jax import lax
from jax.experimental import pallas as pl
from jax.experimental.pallas import tpu as pltpu
from jax.sharding import Mesh
from jax.sharding import PartitionSpec as P

GZ = ("ah", "am", "al", "b", "c")
HIGH = lax.Precision.HIGHEST
F32 = jnp.float32
BF16 = jnp.bfloat16

LANES = 128
DOFS = 64
KINDS = 4
STEPS = 8
CHUNKS = 16
ROWS = STEPS * CHUNKS
PEERS = 64
SLOTS = 6
VMEM = pl.BlockSpec(memory_space=pltpu.VMEM)
SMEM = pl.BlockSpec(memory_space=pltpu.SMEM)


def split(value):
    high = value.astype(BF16)
    return high, (value - high.astype(F32)).astype(BF16)


def doubled(pairs):
    low = lax.broadcasted_iota(jnp.int32, pairs.shape, 1) < DOFS
    turned = pltpu.roll(pairs, DOFS, 1)
    return jnp.concatenate([jnp.where(low, pairs, turned), jnp.where(low, turned, pairs)], axis=0)


def fold(product):
    rows = product.shape[0] // 2
    top, bottom = product[:rows], product[rows:]
    return (top[:, :LANES] + top[:, LANES:]) + (bottom[:, :LANES] + bottom[:, LANES:])


def widened(value, mask_a, mask_b):
    high, low = split(value)
    return jnp.concatenate(
        [
            jnp.concatenate([high * mask_a, high * mask_b], axis=1),
            jnp.concatenate([low * mask_a, low * mask_b], axis=1),
        ],
        axis=0,
    )


def block_of(y, x, flip_y, flip_x):
    return (y ^ flip_y) * 8 + (x ^ flip_x) * 2


def pack_kernel(where_ref, mat_ref, rhs_ref, start_ref, out_ref):
    flip_x, flip_y = where_ref[0], where_ref[1]
    for y in range(4):
        for x in range(4):
            block = block_of(y, x, flip_y, flip_x)
            cell = y * 4 + x
            for p in range(2):
                kind = jnp.full((1, LANES), mat_ref[p, cell].astype(F32))
                for part in range(4):
                    lanes = slice(part * LANES, (part + 1) * LANES)
                    slot = block + (part // 2) * 32 + part % 2
                    out_ref[slot, p : p + 1, :] = rhs_ref[p, cell : cell + 1, lanes]
                    out_ref[slot, 2 + p : 3 + p, :] = start_ref[p, cell : cell + 1, lanes]
                    out_ref[slot, 4 + p : 5 + p, :] = kind


def unpack_kernel(where_ref, in_ref, forward_ref, backward_ref):
    flip_x, flip_y = where_ref[0], where_ref[1]
    for y in range(4):
        for x in range(4):
            block = block_of(y, x, flip_y, flip_x)
            cell = y * 4 + x
            for part in range(4):
                lanes = slice(part * LANES, (part + 1) * LANES)
                slot = block + (part // 2) * 32 + part % 2
                for p in range(2):
                    forward_ref[p, cell : cell + 1, lanes] = in_ref[slot, p : p + 1, :]
                    backward_ref[p, cell : cell + 1, lanes] = in_ref[slot, 2 + p : 3 + p, :]


def arrange_kernel(in_ref, rhs_ref, start_ref, kind_ref):
    for step in range(STEPS):
        for chunk in range(CHUNKS):
            block, p = chunk * 4 + step // 2, step % 2
            row = step * CHUNKS + chunk
            rhs_ref[row : row + 1, :] = in_ref[block, p : p + 1, :]
            start_ref[row : row + 1, :] = in_ref[block, 2 + p : 3 + p, :]
            kind_ref[row : row + 1, :] = in_ref[block, 4 + p : 5 + p, :]


def masks_of(kind):
    half = (lax.broadcasted_iota(jnp.int32, kind.shape, 1) >= DOFS).astype(F32)
    mask_a = jnp.where(kind == half, 1.0, 0.0).astype(BF16)
    mask_b = jnp.where(kind == half + 2.0, 1.0, 0.0).astype(BF16)
    return mask_a, mask_b


def tables_kernel(diag_ref, z_ref, side_ref, kind_ref, tables_ref, mask_a_ref, mask_b_ref, map_f_ref, map_b_ref,
                  plain_ref, run_ref, wide_ref):
    for m in range(KINDS):
        inverse = jnp.concatenate([diag_ref[m], diag_ref[m]], axis=1)
        left = jnp.concatenate([z_ref[m].reshape(2 * DOFS, DOFS), side_ref[m].reshape(4 * DOFS, DOFS)], axis=0)
        joined = jnp.dot(left, inverse, precision=HIGH, preferred_element_type=F32)
        joined = jnp.concatenate([joined, inverse], axis=0)
        high, low = split(joined)
        for q in range(7):
            rows = slice(q * DOFS, (q + 1) * DOFS)
            tables_ref[q, m * DOFS : (m + 1) * DOFS, :LANES] = high[rows]
            tables_ref[q, m * DOFS : (m + 1) * DOFS, LANES:] = low[rows]
        for q in range(2):
            plain_ref[q, m] = joined[q * DOFS : (q + 1) * DOFS]
    mask_a, mask_b = masks_of(kind_ref[...])
    mask_a_ref[...] = mask_a
    mask_b_ref[...] = mask_b

    for q, map_ref in ((0, map_f_ref), (1, map_b_ref)):
        order = list(range(STEPS)) if q == 0 else list(reversed(range(STEPS)))
        for chunk in range(CHUNKS):
            row = order[0] * CHUNKS + chunk
            kind = jnp.broadcast_to(kind_ref[row : row + 1, :], (DOFS, LANES))
            first = jnp.where(kind == 0.0, plain_ref[q, 0], plain_ref[q, 1])
            second = jnp.where(kind == 2.0, plain_ref[q, 2], plain_ref[q, 3])
            run_ref[chunk] = jnp.where(kind < 2.0, first, second)
        for step in order[1:]:
            for group in range(4):
                for k in range(4):
                    chunk = group * 4 + k
                    row = step * CHUNKS + chunk
                    a = jnp.broadcast_to(mask_a[row : row + 1, :], (DOFS, LANES))
                    b = jnp.broadcast_to(mask_b[row : row + 1, :], (DOFS, LANES))
                    wide_ref[k * 2 * DOFS : (k + 1) * 2 * DOFS, :] = widened(run_ref[chunk], a, b)
                product = jnp.dot(wide_ref[...], tables_ref[q], preferred_element_type=F32)
                for k in range(4):
                    run_ref[group * 4 + k] = fold(product[k * 2 * DOFS : (k + 1) * 2 * DOFS])
        for chunk in range(CHUNKS):
            high, low = split(run_ref[chunk])
            map_ref[chunk, :DOFS, :] = high
            map_ref[chunk, DOFS:, :] = low


def chain(const_ref, mask_a_ref, mask_b_ref, table_ref, map_ref, ends_ref, heads_ref, out_ref, descending):
    steps = list(range(STEPS))
    chunks = list(range(CHUNKS))
    if descending:
        steps, chunks = steps[::-1], chunks[::-1]

    def known(step):
        rows = pl.ds(step * CHUNKS, CHUNKS)
        return jnp.concatenate([const_ref[rows, :], const_ref[pl.ds(ROWS + step * CHUNKS, CHUNKS), :]], axis=0)

    def advance(state, step):
        rows = pl.ds(step * CHUNKS, CHUNKS)
        a, b = mask_a_ref[rows, :], mask_b_ref[rows, :]
        wide = widened(state, jnp.concatenate([a, a], axis=0), jnp.concatenate([b, b], axis=0))
        product = jnp.dot(wide, table_ref[...], preferred_element_type=F32)
        return known(step) - fold(product)

    state = known(steps[0])
    for step in steps[1:]:
        state = advance(state, step)
    ends_ref[...] = state

    row = lax.broadcasted_iota(jnp.int32, (8, LANES), 0)
    second = (row & 1) == 1
    rest = (row & 2) == 2
    head = jnp.zeros((8, LANES), F32)
    for chunk in chunks:
        heads_ref[chunk : chunk + 1, :] = head[0:1]
        heads_ref[CHUNKS + chunk : CHUNKS + chunk + 1, :] = head[1:2]
        if chunk == chunks[-1]:
            break
        high = head.astype(BF16).astype(F32)
        wide = jnp.where(rest, head - high, high).astype(BF16)
        product = jnp.dot(wide, map_ref[chunk], preferred_element_type=F32)
        ends = jnp.where(
            second,
            jnp.broadcast_to(ends_ref[CHUNKS + chunk : CHUNKS + chunk + 1, :], (8, LANES)),
            jnp.broadcast_to(ends_ref[chunk : chunk + 1, :], (8, LANES)),
        )
        head = (product + pltpu.roll(product, 2, 0)) + ends

    low = lax.broadcasted_iota(jnp.int32, (CHUNKS, LANES), 1) < DOFS
    state = heads_ref[...]
    for step in steps:
        state = advance(state, step)
        out_ref[pl.ds(step * CHUNKS, CHUNKS), :] = jnp.where(low, state[:CHUNKS], state[CHUNKS:])


def neighbour_terms(wide_ref, pieces, mask_a, mask_b, tables_ref, first):
    for k, piece in enumerate(pieces):
        wide_ref[:, k * 256 : (k + 1) * 256] = widened(doubled(piece), mask_a, mask_b)
    total = None
    for k in range(len(pieces)):
        product = jnp.dot(wide_ref[:, k * 256 : (k + 1) * 256], tables_ref[first + k], preferred_element_type=F32)
        total = product if total is None else total + product
    return fold(total)


def both(mask):
    return jnp.concatenate([mask, mask], axis=0)


def forward_kernel(edge_ref, rhs_ref, start_ref, n0_ref, n1_ref, n2_ref, n3_ref, mask_a_ref, mask_b_ref, tables_ref,
                   map_ref, forward_ref, given_ref, const_ref, ends_ref, heads_ref, wide_ref):
    mask_a, mask_b = both(mask_a_ref[...]), both(mask_b_ref[...])
    start = start_ref[...]
    following = jnp.concatenate([start[1:CHUNKS], jnp.zeros((1, LANES), F32)], axis=0)
    upper = jnp.concatenate([start[CHUNKS:], following], axis=0)
    pieces = [upper]
    for k, ref in enumerate((n0_ref, n1_ref, n2_ref, n3_ref)):
        pieces.append(jnp.where(edge_ref[k] > 0, ref[...], 0.0))
    given = neighbour_terms(wide_ref, pieces, mask_a, mask_b, tables_ref, 1)
    given_ref[...] = given
    own = widened(doubled(rhs_ref[...]), mask_a, mask_b)
    const_ref[...] = fold(jnp.dot(own, tables_ref[6], preferred_element_type=F32)) - given
    chain(const_ref, mask_a_ref, mask_b_ref, tables_ref.at[0], map_ref, ends_ref, heads_ref, forward_ref, False)


def backward_kernel(edge_ref, forward_ref, given_ref, n0_ref, n1_ref, n2_ref, n3_ref, mask_a_ref, mask_b_ref,
                    tables_ref, map_ref, out_ref, const_ref, ends_ref, heads_ref, wide_ref, backward_ref):
    mask_a, mask_b = both(mask_a_ref[...]), both(mask_b_ref[...])
    pieces = []
    for k, ref in enumerate((n0_ref, n1_ref, n2_ref, n3_ref)):
        pieces.append(jnp.where(edge_ref[k] > 0, ref[...], 0.0))
    terms = neighbour_terms(wide_ref, pieces, mask_a, mask_b, tables_ref, 2)
    const_ref[...] = doubled(forward_ref[...]) + (given_ref[...] - terms)
    chain(const_ref, mask_a_ref, mask_b_ref, tables_ref.at[1], map_ref, ends_ref, heads_ref, backward_ref, True)
    for step in range(STEPS):
        for chunk in range(CHUNKS):
            block, p = chunk * 4 + step // 2, step % 2
            row = step * CHUNKS + chunk
            out_ref[block, p : p + 1, :] = forward_ref[row : row + 1, :]
            out_ref[block, 2 + p : 3 + p, :] = backward_ref[row : row + 1, :]
    for block in range(PEERS):
        out_ref[block, 4:6, :] = jnp.zeros((2, LANES), F32)


def shape(*dims, dtype=F32):
    return jax.ShapeDtypeStruct(dims, dtype)


def call(kernel, outs, ins, scratch=(), flops=1000000):
    return pl.pallas_call(
        kernel,
        out_shape=outs,
        in_specs=ins,
        out_specs=jax.tree.map(lambda _: VMEM, outs),
        scratch_shapes=scratch,
        cost_estimate=pl.CostEstimate(flops=flops, bytes_accessed=500000, transcendentals=0),
    )


X_AXES, Y_AXES = ("b", "gx"), ("am", "al", "gy")
RING = [0, 2, 4, 6, 7, 5, 3, 1]


def moved(value, axes, distance):
    pairs = [(RING[i], RING[(i + distance) % 8]) for i in range(8)]
    return lax.ppermute(value, axes, pairs)


def neighbours(value):
    return [
        moved(value, Y_AXES, 1),
        moved(value, Y_AXES, -1),
        moved(value, X_AXES, 1),
        moved(value, X_AXES, -1),
    ]


def per_device(rhs_field, start_field, material, diag_inverse, z_blocks, side_blocks):
    gx, gy = lax.axis_index("gx"), lax.axis_index("gy")
    where = jnp.stack([gx * 3, gy * 3]).astype(jnp.int32)
    x = lax.axis_index("b")
    y = lax.axis_index("am") * 2 + lax.axis_index("al")
    x = jnp.where(gx == 1, 7 - x, x)
    y = jnp.where(gy == 1, 7 - y, y)
    edge = jnp.stack([y > 0, y < 7, x > 0, x < 7]).astype(jnp.int32)

    packed = call(pack_kernel, shape(PEERS, SLOTS, LANES), [SMEM, SMEM, VMEM, VMEM])(
        where, material.reshape(2, 16), rhs_field.reshape(2, 16, 512), start_field.reshape(2, 16, 512)
    )
    arrived = lax.all_to_all(packed, GZ, 0, 0, tiled=True)
    rhs, start, kind = call(
        arrange_kernel, (shape(ROWS, LANES), shape(ROWS, LANES), shape(ROWS, LANES)), [VMEM]
    )(arrived)
    beside = neighbours(start)

    maps = shape(CHUNKS, 2 * DOFS, LANES, dtype=BF16)
    mask = shape(ROWS, LANES, dtype=BF16)
    tables, mask_a, mask_b, map_f, map_b = call(
        tables_kernel,
        (shape(7, 256, 256, dtype=BF16), mask, mask, maps, maps),
        [VMEM] * 4,
        [
            pltpu.VMEM((2, KINDS, DOFS, LANES), F32),
            pltpu.VMEM((CHUNKS, DOFS, LANES), F32),
            pltpu.VMEM((8 * DOFS, 256), BF16),
        ],
        flops=4000000000,
    )(diag_inverse, z_blocks, side_blocks, kind)

    chain_scratch = [
        pltpu.VMEM((2 * ROWS, LANES), F32),
        pltpu.VMEM((2 * CHUNKS, LANES), F32),
        pltpu.VMEM((2 * CHUNKS, LANES), F32),
    ]
    forward, given = call(
        forward_kernel,
        (shape(ROWS, LANES), shape(2 * ROWS, LANES)),
        [SMEM] + [VMEM] * 10,
        chain_scratch + [pltpu.VMEM((4 * ROWS, 5 * 256), BF16)],
        flops=4000000000,
    )(edge, rhs, start, *beside, mask_a, mask_b, tables, map_f)

    beside = neighbours(forward)
    ready = call(
        backward_kernel,
        shape(PEERS, SLOTS, LANES),
        [SMEM] + [VMEM] * 10,
        chain_scratch + [pltpu.VMEM((4 * ROWS, 4 * 256), BF16), pltpu.VMEM((ROWS, LANES), F32)],
        flops=4000000000,
    )(edge, forward, given, *beside, mask_a, mask_b, tables, map_b)
    returned = lax.all_to_all(ready, GZ, 0, 0, tiled=True)
    out_f, out_b = call(unpack_kernel, (shape(2, 16, 512), shape(2, 16, 512)), [SMEM, VMEM])(where, returned)
    return out_f.reshape(rhs_field.shape), out_b.reshape(rhs_field.shape)


def solution(mesh):
    finer = Mesh(
        mesh.devices.reshape(2, 2, 2, 4, 2, mesh.shape["gx"], mesh.shape["gy"]),
        GZ + ("gx", "gy"),
    )
    placed = (P(GZ, "gy", "gx", None), P(GZ, "gy", "gx", None), P(GZ, "gy", "gx"), P(), P(), P())
    return jax.shard_map(
        per_device,
        mesh=finer,
        in_specs=placed,
        out_specs=(P(GZ, "gy", "gx", None), P(GZ, "gy", "gx", None)),
        check_vma=False,
    )
```

```python
import functools

import jax
import jax.numpy as jnp
from jax import lax
from jax.experimental import pallas as pl
from jax.experimental.pallas import tpu as pltpu
from jax.sharding import Mesh
from jax.sharding import PartitionSpec as P

GZ = ("ah", "am", "al", "b", "c")
HIGH = lax.Precision.HIGHEST
F32 = jnp.float32
BF16 = jnp.bfloat16

LANES = 128
DOFS = 64
KINDS = 4
STEPS = 8
CHUNKS = 16
ROWS = STEPS * CHUNKS
PEERS = 64
SLOTS = 6
VMEM = pl.BlockSpec(memory_space=pltpu.VMEM)
SMEM = pl.BlockSpec(memory_space=pltpu.SMEM)


def split(value):
    high = value.astype(BF16)
    return high, (value - high.astype(F32)).astype(BF16)


def doubled(pairs):
    low = lax.broadcasted_iota(jnp.int32, pairs.shape, 1) < DOFS
    turned = pltpu.roll(pairs, DOFS, 1)
    return jnp.concatenate([jnp.where(low, pairs, turned), jnp.where(low, turned, pairs)], axis=0)


def fold(product):
    rows = product.shape[0] // 2
    top, bottom = product[:rows], product[rows:]
    return (top[:, :LANES] + top[:, LANES:]) + (bottom[:, :LANES] + bottom[:, LANES:])


def widened(value, mask_a, mask_b):
    high, low = split(value)
    return jnp.concatenate(
        [
            jnp.concatenate([high * mask_a, high * mask_b], axis=1),
            jnp.concatenate([low * mask_a, low * mask_b], axis=1),
        ],
        axis=0,
    )


def block_of(y, x, flip_y, flip_x):
    return (y ^ flip_y) * 8 + (x ^ flip_x) * 2


def flips():
    return lax.axis_index("gx") * 3, lax.axis_index("gy") * 3


def pack_kernel(mat_ref, rhs_ref, start_ref, out_ref):
    flip_x, flip_y = flips()
    for y in range(4):
        for x in range(4):
            block = block_of(y, x, flip_y, flip_x)
            for p in range(2):
                kind = jnp.full((1, LANES), mat_ref[p, y, x].astype(F32))
                for part in range(4):
                    lanes = slice(part * LANES, (part + 1) * LANES)
                    slot = block + (part // 2) * 32 + part % 2
                    out_ref[slot, p : p + 1, :] = rhs_ref[p, y, x : x + 1, lanes]
                    out_ref[slot, 2 + p : 3 + p, :] = start_ref[p, y, x : x + 1, lanes]
                    out_ref[slot, 4 + p : 5 + p, :] = kind


def unpack_kernel(in_ref, forward_ref, backward_ref):
    flip_x, flip_y = flips()
    for y in range(4):
        for x in range(4):
            block = block_of(y, x, flip_y, flip_x)
            for part in range(4):
                lanes = slice(part * LANES, (part + 1) * LANES)
                slot = block + (part // 2) * 32 + part % 2
                for p in range(2):
                    forward_ref[p, y, x : x + 1, lanes] = in_ref[slot, p : p + 1, :]
                    backward_ref[p, y, x : x + 1, lanes] = in_ref[slot, 2 + p : 3 + p, :]


def masks_of(kind):
    half = (lax.broadcasted_iota(jnp.int32, kind.shape, 1) >= DOFS).astype(F32)
    mask_a = jnp.where(kind == half, 1.0, 0.0).astype(BF16)
    mask_b = jnp.where(kind == half + 2.0, 1.0, 0.0).astype(BF16)
    return mask_a, mask_b


def arrange_kernel(in_ref, rhs_ref, start_ref, kind_ref, mask_a_ref, mask_b_ref):
    for step in range(STEPS):
        for chunk in range(CHUNKS):
            block, p = chunk * 4 + step // 2, step % 2
            row = step * CHUNKS + chunk
            rhs_ref[row : row + 1, :] = in_ref[block, p : p + 1, :]
            start_ref[row : row + 1, :] = in_ref[block, 2 + p : 3 + p, :]
            kind_ref[row : row + 1, :] = in_ref[block, 4 + p : 5 + p, :]
    mask_a, mask_b = masks_of(kind_ref[...])
    mask_a_ref[...] = mask_a
    mask_b_ref[...] = mask_b


def tables_kernel(diag_ref, z_ref, side_ref, tables_ref, plain_ref):
    for m in range(KINDS):
        inverse = jnp.concatenate([diag_ref[m], diag_ref[m]], axis=1)
        left = jnp.concatenate([z_ref[m].reshape(2 * DOFS, DOFS), side_ref[m].reshape(4 * DOFS, DOFS)], axis=0)
        joined = jnp.dot(left, inverse, precision=HIGH, preferred_element_type=F32)
        joined = jnp.concatenate([joined, inverse], axis=0)
        high, low = split(joined)
        for q in range(7):
            rows = slice(q * DOFS, (q + 1) * DOFS)
            tables_ref[q, m * DOFS : (m + 1) * DOFS, :LANES] = high[rows]
            tables_ref[q, m * DOFS : (m + 1) * DOFS, LANES:] = low[rows]
        for q in range(2):
            plain_ref[q, m] = joined[q * DOFS : (q + 1) * DOFS]


def maps_kernel(q, kind_ref, mask_a_ref, mask_b_ref, tables_ref, plain_ref, after_ref, map_ref, run_ref, wide_ref):
    order = list(range(STEPS)) if q == 0 else list(reversed(range(STEPS)))
    for chunk in range(CHUNKS):
        row = order[0] * CHUNKS + chunk
        kind = jnp.broadcast_to(kind_ref[row : row + 1, :], (DOFS, LANES))
        first = jnp.where(kind == 0.0, plain_ref[q, 0], plain_ref[q, 1])
        second = jnp.where(kind == 2.0, plain_ref[q, 2], plain_ref[q, 3])
        run_ref[chunk] = jnp.where(kind < 2.0, first, second)
    for step in order[1:]:
        rows = pl.ds(step * CHUNKS, CHUNKS)
        mask_a, mask_b = mask_a_ref[rows, :], mask_b_ref[rows, :]
        for group in range(4):
            for k in range(4):
                chunk = group * 4 + k
                a = jnp.broadcast_to(mask_a[chunk : chunk + 1, :], (DOFS, LANES))
                b = jnp.broadcast_to(mask_b[chunk : chunk + 1, :], (DOFS, LANES))
                wide_ref[k * 2 * DOFS : (k + 1) * 2 * DOFS, :] = widened(run_ref[chunk], a, b)
            product = jnp.dot(wide_ref[...], tables_ref[q], preferred_element_type=F32)
            for k in range(4):
                run_ref[group * 4 + k] = fold(product[k * 2 * DOFS : (k + 1) * 2 * DOFS])
    for chunk in range(CHUNKS):
        high, low = split(run_ref[chunk])
        map_ref[chunk, :DOFS, :] = high
        map_ref[chunk, DOFS:, :] = low


def chain(const_ref, mask_a_ref, mask_b_ref, table_ref, map_ref, ends_ref, heads_ref, out_ref, descending):
    steps = list(range(STEPS))
    chunks = list(range(CHUNKS))
    if descending:
        steps, chunks = steps[::-1], chunks[::-1]

    def known(step):
        rows = pl.ds(step * CHUNKS, CHUNKS)
        return jnp.concatenate([const_ref[rows, :], const_ref[pl.ds(ROWS + step * CHUNKS, CHUNKS), :]], axis=0)

    def advance(state, step):
        rows = pl.ds(step * CHUNKS, CHUNKS)
        a, b = mask_a_ref[rows, :], mask_b_ref[rows, :]
        wide = widened(state, jnp.concatenate([a, a], axis=0), jnp.concatenate([b, b], axis=0))
        product = jnp.dot(wide, table_ref[...], preferred_element_type=F32)
        return known(step) - fold(product)

    state = known(steps[0])
    for step in steps[1:]:
        state = advance(state, step)
    ends_ref[...] = state

    row = lax.broadcasted_iota(jnp.int32, (8, LANES), 0)
    second = (row & 1) == 1
    rest = (row & 2) == 2
    head = jnp.zeros((8, LANES), F32)
    for chunk in chunks:
        heads_ref[chunk : chunk + 1, :] = head[0:1]
        heads_ref[CHUNKS + chunk : CHUNKS + chunk + 1, :] = head[1:2]
        if chunk == chunks[-1]:
            break
        high = head.astype(BF16).astype(F32)
        wide = jnp.where(rest, head - high, high).astype(BF16)
        product = jnp.dot(wide, map_ref[chunk], preferred_element_type=F32)
        ends = jnp.where(
            second,
            jnp.broadcast_to(ends_ref[CHUNKS + chunk : CHUNKS + chunk + 1, :], (8, LANES)),
            jnp.broadcast_to(ends_ref[chunk : chunk + 1, :], (8, LANES)),
        )
        head = (product + pltpu.roll(product, 2, 0)) + ends

    low = lax.broadcasted_iota(jnp.int32, (CHUNKS, LANES), 1) < DOFS
    state = heads_ref[...]
    for step in steps:
        state = advance(state, step)
        out_ref[pl.ds(step * CHUNKS, CHUNKS), :] = jnp.where(low, state[:CHUNKS], state[CHUNKS:])


def beside_inside(refs):
    x, y = lax.axis_index("b"), lax.axis_index("am") * 2 + lax.axis_index("al")
    x = jnp.where(lax.axis_index("gx") == 1, 7 - x, x)
    y = jnp.where(lax.axis_index("gy") == 1, 7 - y, y)
    inside = (y > 0, y < 7, x > 0, x < 7)
    return [jnp.where(here, ref[...], 0.0) for here, ref in zip(inside, refs)]


def neighbour_terms(wide_ref, pieces, mask_a, mask_b, tables_ref, first):
    for k, piece in enumerate(pieces):
        wide_ref[:, k * 256 : (k + 1) * 256] = widened(doubled(piece), mask_a, mask_b)
    total = None
    for k in range(len(pieces)):
        product = jnp.dot(wide_ref[:, k * 256 : (k + 1) * 256], tables_ref[first + k], preferred_element_type=F32)
        total = product if total is None else total + product
    return fold(total)


def both(mask):
    return jnp.concatenate([mask, mask], axis=0)


def forward_kernel(rhs_ref, start_ref, n0_ref, n1_ref, n2_ref, n3_ref, mask_a_ref, mask_b_ref, tables_ref,
                   map_ref, forward_ref, given_ref, const_ref, ends_ref, heads_ref, wide_ref):
    mask_a, mask_b = both(mask_a_ref[...]), both(mask_b_ref[...])
    start = start_ref[...]
    following = jnp.concatenate([start[1:CHUNKS], jnp.zeros((1, LANES), F32)], axis=0)
    upper = jnp.concatenate([start[CHUNKS:], following], axis=0)
    pieces = [upper] + beside_inside((n0_ref, n1_ref, n2_ref, n3_ref))
    given = neighbour_terms(wide_ref, pieces, mask_a, mask_b, tables_ref, 1)
    given_ref[...] = given
    own = widened(doubled(rhs_ref[...]), mask_a, mask_b)
    const_ref[...] = fold(jnp.dot(own, tables_ref[6], preferred_element_type=F32)) - given
    chain(const_ref, mask_a_ref, mask_b_ref, tables_ref.at[0], map_ref, ends_ref, heads_ref, forward_ref, False)


def backward_kernel(forward_ref, given_ref, n0_ref, n1_ref, n2_ref, n3_ref, mask_a_ref, mask_b_ref,
                    tables_ref, map_ref, out_ref, const_ref, ends_ref, heads_ref, wide_ref, backward_ref):
    mask_a, mask_b = both(mask_a_ref[...]), both(mask_b_ref[...])
    pieces = beside_inside((n0_ref, n1_ref, n2_ref, n3_ref))
    terms = neighbour_terms(wide_ref, pieces, mask_a, mask_b, tables_ref, 2)
    const_ref[...] = doubled(forward_ref[...]) + (given_ref[...] - terms)
    chain(const_ref, mask_a_ref, mask_b_ref, tables_ref.at[1], map_ref, ends_ref, heads_ref, backward_ref, True)
    for step in range(STEPS):
        for chunk in range(CHUNKS):
            block, p = chunk * 4 + step // 2, step % 2
            row = step * CHUNKS + chunk
            out_ref[block, p : p + 1, :] = forward_ref[row : row + 1, :]
            out_ref[block, 2 + p : 3 + p, :] = backward_ref[row : row + 1, :]
    for block in range(PEERS):
        out_ref[block, 4:6, :] = jnp.zeros((2, LANES), F32)


def shape(*dims, dtype=F32):
    return jax.ShapeDtypeStruct(dims, dtype)


def call(kernel, outs, ins, scratch=(), flops=1000000):
    return pl.pallas_call(
        kernel,
        out_shape=outs,
        in_specs=ins,
        out_specs=jax.tree.map(lambda _: VMEM, outs),
        scratch_shapes=scratch,
        cost_estimate=pl.CostEstimate(flops=flops, bytes_accessed=500000, transcendentals=0),
        compiler_params=pltpu.CompilerParams(vmem_limit_bytes=16 * 1024 * 1024),
    )


X_AXES, Y_AXES = ("b", "gx"), ("am", "al", "gy")
RING = [0, 2, 4, 6, 7, 5, 3, 1]


def moved(value, axes, distance):
    pairs = [(RING[i], RING[(i + distance) % 8]) for i in range(8)]
    return lax.ppermute(value, axes, pairs)


def neighbours(value):
    return [
        moved(value, Y_AXES, 1),
        moved(value, Y_AXES, -1),
        moved(value, X_AXES, 1),
        moved(value, X_AXES, -1),
    ]


def per_device(rhs_field, start_field, material, diag_inverse, z_blocks, side_blocks):
    mask = shape(ROWS, LANES, dtype=BF16)
    field = shape(ROWS, LANES)
    packed = call(pack_kernel, shape(PEERS, SLOTS, LANES), [SMEM, VMEM, VMEM])(material, rhs_field, start_field)
    arrived = lax.all_to_all(packed, GZ, 0, 0, tiled=True)
    tables, plain = call(
        tables_kernel,
        (shape(7, 256, 256, dtype=BF16), shape(2, KINDS, DOFS, LANES)),
        [VMEM] * 3,
        flops=4000000000,
    )(diag_inverse, z_blocks, side_blocks)
    rhs, start, kind, mask_a, mask_b = call(arrange_kernel, (field, field, field, mask, mask), [VMEM])(arrived)
    beside = neighbours(start)

    def maps(q, after):
        return call(
            functools.partial(maps_kernel, q),
            shape(CHUNKS, 2 * DOFS, LANES, dtype=BF16),
            [VMEM] * 5 + [pl.BlockSpec(memory_space=pl.ANY)],
            [pltpu.VMEM((CHUNKS, DOFS, LANES), F32), pltpu.VMEM((8 * DOFS, 256), BF16)],
            flops=4000000000,
        )(kind, mask_a, mask_b, tables, plain, after)

    map_f = maps(0, start)
    chain_scratch = [
        pltpu.VMEM((2 * ROWS, LANES), F32),
        pltpu.VMEM((2 * CHUNKS, LANES), F32),
        pltpu.VMEM((2 * CHUNKS, LANES), F32),
    ]
    forward, given = call(
        forward_kernel,
        (field, shape(2 * ROWS, LANES)),
        [VMEM] * 10,
        chain_scratch + [pltpu.VMEM((4 * ROWS, 5 * 256), BF16)],
        flops=4000000000,
    )(rhs, start, *beside, mask_a, mask_b, tables, map_f)

    beside = neighbours(forward)
    map_b = maps(1, forward)
    ready = call(
        backward_kernel,
        shape(PEERS, SLOTS, LANES),
        [VMEM] * 10,
        chain_scratch + [pltpu.VMEM((4 * ROWS, 4 * 256), BF16), pltpu.VMEM((ROWS, LANES), F32)],
        flops=4000000000,
    )(forward, given, *beside, mask_a, mask_b, tables, map_b)
    returned = lax.all_to_all(ready, GZ, 0, 0, tiled=True)
    cells = shape(*rhs_field.shape)
    return call(unpack_kernel, (cells, cells), [VMEM])(returned)


def solution(mesh):
    finer = Mesh(
        mesh.devices.reshape(2, 2, 2, 4, 2, mesh.shape["gx"], mesh.shape["gy"]),
        GZ + ("gx", "gy"),
    )
    placed = (P(GZ, "gy", "gx", None), P(GZ, "gy", "gx", None), P(GZ, "gy", "gx"), P(), P(), P())
    return jax.shard_map(
        per_device,
        mesh=finer,
        in_specs=placed,
        out_specs=(P(GZ, "gy", "gx", None), P(GZ, "gy", "gx", None)),
        check_vma=False,
    )
```

```python
import functools

import jax
import jax.numpy as jnp
from jax import lax
from jax.experimental import pallas as pl
from jax.experimental.pallas import tpu as pltpu
from jax.sharding import Mesh
from jax.sharding import PartitionSpec as P

GZ = ("ah", "am", "al", "b", "c")
HIGH = lax.Precision.HIGHEST
F32 = jnp.float32
BF16 = jnp.bfloat16

LANES = 128
DOFS = 64
KINDS = 4
STEPS = 4
CHUNKS = 128 // STEPS
ROWS = STEPS * CHUNKS
PEERS = 64
SLOTS = 6
VMEM = pl.BlockSpec(memory_space=pltpu.VMEM)
HBM = pl.BlockSpec(memory_space=pltpu.HBM)


def split(value):
    high = value.astype(BF16)
    return high, (value - high.astype(F32)).astype(BF16)


def doubled(pairs):
    low = lax.broadcasted_iota(jnp.int32, pairs.shape, 1) < DOFS
    turned = pltpu.roll(pairs, DOFS, 1)
    return jnp.concatenate([jnp.where(low, pairs, turned), jnp.where(low, turned, pairs)], axis=0)


def fold(product):
    rows = product.shape[0] // 2
    top, bottom = product[:rows], product[rows:]
    return (top[:, :LANES] + top[:, LANES:]) + (bottom[:, :LANES] + bottom[:, LANES:])


def widened(value, mask_a, mask_b):
    high, low = split(value)
    return jnp.concatenate(
        [
            jnp.concatenate([high * mask_a, high * mask_b], axis=1),
            jnp.concatenate([low * mask_a, low * mask_b], axis=1),
        ],
        axis=0,
    )


def block_of(y, x, flip_y, flip_x):
    return (y ^ flip_y) * 8 + (x ^ flip_x) * 2


def flips():
    return lax.axis_index("gx") * 3, lax.axis_index("gy") * 3


def pack(mat_ref, rhs_ref, start_ref, out_ref):
    flip_x, flip_y = flips()
    for y in range(4):
        for x in range(4):
            block = block_of(y, x, flip_y, flip_x)
            for p in range(2):
                kind = jnp.full((1, LANES), mat_ref[p, y, x].astype(F32))
                for part in range(4):
                    lanes = slice(part * LANES, (part + 1) * LANES)
                    slot = block + (part // 2) * 32 + part % 2
                    out_ref[slot, p : p + 1, :] = rhs_ref[p, y, x : x + 1, lanes]
                    out_ref[slot, 2 + p : 3 + p, :] = start_ref[p, y, x : x + 1, lanes]
                    out_ref[slot, 4 + p : 5 + p, :] = kind


def pack_kernel(mat_hbm, rhs_hbm, start_hbm, out_ref, mat_ref, rhs_ref, start_ref, sems):
    copies = [
        pltpu.make_async_copy(source, target, sems.at[k])
        for k, (source, target) in enumerate(((mat_hbm, mat_ref), (rhs_hbm, rhs_ref), (start_hbm, start_ref)))
    ]
    for copy in copies:
        copy.start()
    for copy in copies:
        copy.wait()
    pack(mat_ref, rhs_ref, start_ref, out_ref)


def unpack_kernel(in_ref, forward_ref, backward_ref):
    flip_x, flip_y = flips()
    for y in range(4):
        for x in range(4):
            block = block_of(y, x, flip_y, flip_x)
            for part in range(4):
                lanes = slice(part * LANES, (part + 1) * LANES)
                slot = block + (part // 2) * 32 + part % 2
                for p in range(2):
                    forward_ref[p, y, x : x + 1, lanes] = in_ref[slot, p : p + 1, :]
                    backward_ref[p, y, x : x + 1, lanes] = in_ref[slot, 2 + p : 3 + p, :]


def masks_of(kind):
    half = (lax.broadcasted_iota(jnp.int32, kind.shape, 1) >= DOFS).astype(F32)
    mask_a = jnp.where(kind == half, 1.0, 0.0).astype(BF16)
    mask_b = jnp.where(kind == half + 2.0, 1.0, 0.0).astype(BF16)
    return mask_a, mask_b


def arrange_kernel(in_ref, rhs_ref, start_ref, kind_ref, mask_a_ref, mask_b_ref):
    for step in range(STEPS):
        for chunk in range(CHUNKS):
            block, p = chunk * (STEPS // 2) + step // 2, step % 2
            row = step * CHUNKS + chunk
            rhs_ref[row : row + 1, :] = in_ref[block, p : p + 1, :]
            start_ref[row : row + 1, :] = in_ref[block, 2 + p : 3 + p, :]
            kind_ref[row : row + 1, :] = in_ref[block, 4 + p : 5 + p, :]
    mask_a, mask_b = masks_of(kind_ref[...])
    mask_a_ref[...] = mask_a
    mask_b_ref[...] = mask_b


def tables_kernel(diag_ref, z_ref, side_ref, tables_ref, plain_ref):
    for m in range(KINDS):
        inverse = jnp.concatenate([diag_ref[m], diag_ref[m]], axis=1)
        left = jnp.concatenate([z_ref[m].reshape(2 * DOFS, DOFS), side_ref[m].reshape(4 * DOFS, DOFS)], axis=0)
        joined = jnp.dot(left, inverse, precision=HIGH, preferred_element_type=F32)
        joined = jnp.concatenate([joined, inverse], axis=0)
        high, low = split(joined)
        for q in range(7):
            rows = slice(q * DOFS, (q + 1) * DOFS)
            tables_ref[q, m * DOFS : (m + 1) * DOFS, :LANES] = high[rows]
            tables_ref[q, m * DOFS : (m + 1) * DOFS, LANES:] = low[rows]
        for q in range(2):
            plain_ref[q, m] = joined[q * DOFS : (q + 1) * DOFS]


def chain_order(descending):
    steps, chunks = list(range(STEPS)), list(range(CHUNKS))
    return (steps[::-1], chunks[::-1]) if descending else (steps, chunks)


def maps_kernel(q, kind_ref, mask_a_ref, mask_b_ref, tables_ref, plain_ref, after_ref, map_ref, run_ref, wide_ref):
    order = chain_order(q == 1)[0]
    for chunk in range(CHUNKS):
        row = order[0] * CHUNKS + chunk
        kind = jnp.broadcast_to(kind_ref[row : row + 1, :], (DOFS, LANES))
        first = jnp.where(kind == 0.0, plain_ref[q, 0], plain_ref[q, 1])
        second = jnp.where(kind == 2.0, plain_ref[q, 2], plain_ref[q, 3])
        run_ref[chunk] = jnp.where(kind < 2.0, first, second)
    for step in order[1:]:
        rows = pl.ds(step * CHUNKS, CHUNKS)
        mask_a, mask_b = mask_a_ref[rows, :], mask_b_ref[rows, :]
        for group in range(CHUNKS // 4):
            for k in range(4):
                chunk = group * 4 + k
                a = jnp.broadcast_to(mask_a[chunk : chunk + 1, :], (DOFS, LANES))
                b = jnp.broadcast_to(mask_b[chunk : chunk + 1, :], (DOFS, LANES))
                wide_ref[k * 2 * DOFS : (k + 1) * 2 * DOFS, :] = widened(run_ref[chunk], a, b)
            product = jnp.dot(wide_ref[...], tables_ref[q], preferred_element_type=F32)
            for k in range(4):
                run_ref[group * 4 + k] = fold(product[k * 2 * DOFS : (k + 1) * 2 * DOFS])
    for place, chunk in enumerate(chain_order(q == 1)[1]):
        product = run_ref[chunk]
        if place % 2 == 1:
            turned = product.T[:DOFS]
            product = jnp.concatenate([turned, turned], axis=1)
        map_ref[chunk] = product


def both(mask):
    return jnp.concatenate([mask, mask], axis=0)


def pairs_of(state):
    low = lax.broadcasted_iota(jnp.int32, (CHUNKS, LANES), 1) < DOFS
    return jnp.where(low, state[:CHUNKS], state[CHUNKS:])


def chain(const_ref, mask_a_ref, mask_b_ref, table_ref, map_ref, ends_ref, heads_ref, out_ref, descending):
    steps, chunks = chain_order(descending)

    def known(step):
        rows = pl.ds(step * CHUNKS, CHUNKS)
        return jnp.concatenate([const_ref[rows, :], const_ref[pl.ds(ROWS + step * CHUNKS, CHUNKS), :]], axis=0)

    def advance(state, step):
        rows = pl.ds(step * CHUNKS, CHUNKS)
        wide = widened(state, both(mask_a_ref[rows, :]), both(mask_b_ref[rows, :]))
        product = jnp.dot(wide, table_ref[...], preferred_element_type=F32)
        return known(step) - fold(product)

    state = known(steps[0])
    for step in steps[1:]:
        state = advance(state, step)
    ends_ref[...] = pairs_of(state)

    row = lax.broadcasted_iota(jnp.int32, (DOFS, LANES), 0)
    lane = lax.broadcasted_iota(jnp.int32, (DOFS, LANES), 1)
    low = lane < DOFS
    unit = jnp.where((lane & (DOFS - 1)) == row, 1.0, 0.0)
    upright = jnp.zeros((DOFS, LANES), F32)
    for place, chunk in enumerate(chunks):
        end = ends_ref[chunk : chunk + 1, :]
        if place % 2 == 0:
            heads_ref[chunk : chunk + 1, :] = jnp.sum(upright * unit, axis=0, keepdims=True)
            flat = jnp.sum(upright * map_ref[chunk], axis=0, keepdims=True) + end
        else:
            heads_ref[chunk : chunk + 1, :] = flat
            terms = flat * map_ref[chunk] + end * unit
            first = jnp.sum(jnp.where(low, terms, 0.0), axis=1, keepdims=True)
            second = jnp.sum(jnp.where(low, 0.0, terms), axis=1, keepdims=True)
            upright = jnp.where(low, first, second)

    state = doubled(heads_ref[...])
    for step in steps:
        state = advance(state, step)
        out_ref[pl.ds(step * CHUNKS, CHUNKS), :] = pairs_of(state)


def beside_inside(refs):
    x, y = lax.axis_index("b"), lax.axis_index("am") * 2 + lax.axis_index("al")
    x = jnp.where(lax.axis_index("gx") == 1, 7 - x, x)
    y = jnp.where(lax.axis_index("gy") == 1, 7 - y, y)
    inside = (y > 0, y < 7, x > 0, x < 7)
    return [jnp.where(here, ref[...], 0.0) for here, ref in zip(inside, refs)]


def neighbour_terms(wide_ref, pieces, mask_a, mask_b, tables_ref, first):
    for k, piece in enumerate(pieces):
        wide_ref[:, k * 256 : (k + 1) * 256] = widened(doubled(piece), mask_a, mask_b)
    total = None
    for k in range(len(pieces)):
        product = jnp.dot(wide_ref[:, k * 256 : (k + 1) * 256], tables_ref[first + k], preferred_element_type=F32)
        total = product if total is None else total + product
    return fold(total)


def forward_kernel(rhs_ref, start_ref, n0_ref, n1_ref, n2_ref, n3_ref, mask_a_ref, mask_b_ref, tables_ref,
                   map_ref, forward_ref, given_ref, const_ref, ends_ref, heads_ref, wide_ref):
    mask_a, mask_b = both(mask_a_ref[...]), both(mask_b_ref[...])
    start = start_ref[...]
    following = jnp.concatenate([start[1:CHUNKS], jnp.zeros((1, LANES), F32)], axis=0)
    upper = jnp.concatenate([start[CHUNKS:], following], axis=0)
    pieces = [upper] + beside_inside((n0_ref, n1_ref, n2_ref, n3_ref))
    given = neighbour_terms(wide_ref, pieces, mask_a, mask_b, tables_ref, 1)
    given_ref[...] = given
    own = widened(doubled(rhs_ref[...]), mask_a, mask_b)
    const_ref[...] = fold(jnp.dot(own, tables_ref[6], preferred_element_type=F32)) - given
    chain(const_ref, mask_a_ref, mask_b_ref, tables_ref.at[0], map_ref, ends_ref, heads_ref, forward_ref, False)


def backward_kernel(forward_ref, given_ref, n0_ref, n1_ref, n2_ref, n3_ref, mask_a_ref, mask_b_ref,
                    tables_ref, map_ref, out_ref, const_ref, ends_ref, heads_ref, wide_ref, backward_ref):
    mask_a, mask_b = both(mask_a_ref[...]), both(mask_b_ref[...])
    pieces = beside_inside((n0_ref, n1_ref, n2_ref, n3_ref))
    terms = neighbour_terms(wide_ref, pieces, mask_a, mask_b, tables_ref, 2)
    const_ref[...] = doubled(forward_ref[...]) + (given_ref[...] - terms)
    chain(const_ref, mask_a_ref, mask_b_ref, tables_ref.at[1], map_ref, ends_ref, heads_ref, backward_ref, True)
    for step in range(STEPS):
        for chunk in range(CHUNKS):
            block, p = chunk * (STEPS // 2) + step // 2, step % 2
            row = step * CHUNKS + chunk
            out_ref[block, p : p + 1, :] = forward_ref[row : row + 1, :]
            out_ref[block, 2 + p : 3 + p, :] = backward_ref[row : row + 1, :]
    for block in range(PEERS):
        out_ref[block, 4:6, :] = jnp.zeros((2, LANES), F32)


def shape(*dims, dtype=F32):
    return jax.ShapeDtypeStruct(dims, dtype)


def call(kernel, outs, ins, scratch=(), flops=1000000, limit=16 * 1024 * 1024):
    return pl.pallas_call(
        kernel,
        out_shape=outs,
        in_specs=ins,
        out_specs=jax.tree.map(lambda _: VMEM, outs),
        scratch_shapes=scratch,
        cost_estimate=pl.CostEstimate(flops=flops, bytes_accessed=500000, transcendentals=0),
        compiler_params=pltpu.CompilerParams(vmem_limit_bytes=limit),
    )


X_AXES, Y_AXES = ("b", "gx"), ("am", "al", "gy")
RING = [0, 2, 4, 6, 7, 5, 3, 1]


def moved(value, axes, distance):
    pairs = [(RING[i], RING[(i + distance) % 8]) for i in range(8)]
    return lax.ppermute(value, axes, pairs)


def neighbours(value):
    return [
        moved(value, Y_AXES, 1),
        moved(value, Y_AXES, -1),
        moved(value, X_AXES, 1),
        moved(value, X_AXES, -1),
    ]


def per_device(rhs_field, start_field, material, diag_inverse, z_blocks, side_blocks):
    mask = shape(ROWS, LANES, dtype=BF16)
    field = shape(ROWS, LANES)
    packed = call(
        pack_kernel,
        shape(PEERS, SLOTS, LANES),
        [HBM] * 3,
        [
            pltpu.SMEM(material.shape, jnp.int32),
            pltpu.VMEM(rhs_field.shape, F32),
            pltpu.VMEM(rhs_field.shape, F32),
            pltpu.SemaphoreType.DMA((3,)),
        ],
        limit=None,
    )(material, rhs_field, start_field)
    arrived = lax.all_to_all(packed, GZ, 0, 0, tiled=True)
    tables, plain = call(
        tables_kernel,
        (shape(7, 256, 256, dtype=BF16), shape(2, KINDS, DOFS, LANES)),
        [VMEM] * 3,
        flops=4000000000,
    )(diag_inverse, z_blocks, side_blocks)
    rhs, start, kind, mask_a, mask_b = call(arrange_kernel, (field, field, field, mask, mask), [VMEM])(arrived)
    beside = neighbours(start)

    def maps(q, after):
        return call(
            functools.partial(maps_kernel, q),
            shape(CHUNKS, DOFS, LANES),
            [VMEM] * 5 + [pl.BlockSpec(memory_space=pl.ANY)],
            [pltpu.VMEM((CHUNKS, DOFS, LANES), F32), pltpu.VMEM((8 * DOFS, 256), BF16)],
            flops=4000000000,
        )(kind, mask_a, mask_b, tables, plain, after)

    map_f = maps(0, start)
    chain_scratch = [
        pltpu.VMEM((2 * ROWS, LANES), F32),
        pltpu.VMEM((CHUNKS, LANES), F32),
        pltpu.VMEM((CHUNKS, LANES), F32),
    ]
    forward, given = call(
        forward_kernel,
        (field, shape(2 * ROWS, LANES)),
        [VMEM] * 10,
        chain_scratch + [pltpu.VMEM((4 * ROWS, 5 * 256), BF16)],
        flops=4000000000,
    )(rhs, start, *beside, mask_a, mask_b, tables, map_f)

    beside = neighbours(forward)
    map_b = maps(1, forward)
    ready = call(
        backward_kernel,
        shape(PEERS, SLOTS, LANES),
        [VMEM] * 10,
        chain_scratch + [pltpu.VMEM((4 * ROWS, 4 * 256), BF16), pltpu.VMEM((ROWS, LANES), F32)],
        flops=4000000000,
    )(forward, given, *beside, mask_a, mask_b, tables, map_b)
    returned = lax.all_to_all(ready, GZ, 0, 0, tiled=True)
    cells = shape(*rhs_field.shape)
    return call(unpack_kernel, (cells, cells), [VMEM])(returned)


def solution(mesh):
    finer = Mesh(
        mesh.devices.reshape(2, 2, 2, 4, 2, mesh.shape["gx"], mesh.shape["gy"]),
        GZ + ("gx", "gy"),
    )
    placed = (P(GZ, "gy", "gx", None), P(GZ, "gy", "gx", None), P(GZ, "gy", "gx"), P(), P(), P())
    return jax.shard_map(
        per_device,
        mesh=finer,
        in_specs=placed,
        out_specs=(P(GZ, "gy", "gx", None), P(GZ, "gy", "gx", None)),
        check_vma=False,
    )
```

```python
import functools

import jax
import jax.numpy as jnp
from jax import lax
from jax.experimental import pallas as pl
from jax.experimental.pallas import tpu as pltpu
from jax.sharding import Mesh
from jax.sharding import PartitionSpec as P

GZ = ("ah", "am", "al", "b", "c")
HIGH = lax.Precision.HIGHEST
F32 = jnp.float32
BF16 = jnp.bfloat16

LANES = 128
DOFS = 64
KINDS = 4
STEPS = 4
CHUNKS = 128 // STEPS
ROWS = STEPS * CHUNKS
PEERS = 64
SLOTS = 5
VMEM = pl.BlockSpec(memory_space=pltpu.VMEM)
HBM = pl.BlockSpec(memory_space=pltpu.HBM)


def split(value):
    high = value.astype(BF16)
    return high, (value - high.astype(F32)).astype(BF16)


def doubled(pairs):
    low = lax.broadcasted_iota(jnp.int32, pairs.shape, 1) < DOFS
    turned = pltpu.roll(pairs, DOFS, 1)
    return jnp.concatenate([jnp.where(low, pairs, turned), jnp.where(low, turned, pairs)], axis=0)


def fold(product):
    rows = product.shape[0] // 2
    top, bottom = product[:rows], product[rows:]
    return (top[:, :LANES] + top[:, LANES:]) + (bottom[:, :LANES] + bottom[:, LANES:])


def widened(value, mask_a, mask_b):
    high, low = split(value)
    return jnp.concatenate(
        [
            jnp.concatenate([high * mask_a, high * mask_b], axis=1),
            jnp.concatenate([low * mask_a, low * mask_b], axis=1),
        ],
        axis=0,
    )


def block_of(y, x, flip_y, flip_x):
    return (y ^ flip_y) * 8 + (x ^ flip_x) * 2


def flips():
    return lax.axis_index("gx") * 3, lax.axis_index("gy") * 3


def pack(mat_ref, rhs_ref, start_ref, out_ref):
    flip_x, flip_y = flips()
    low = lax.broadcasted_iota(jnp.int32, (1, LANES), 1) < DOFS
    for y in range(4):
        for x in range(4):
            block = block_of(y, x, flip_y, flip_x)
            kinds = jnp.where(low, mat_ref[0, y, x].astype(F32), mat_ref[1, y, x].astype(F32))
            for part in range(4):
                out_ref[block + (part // 2) * 32 + part % 2, 4:5, :] = kinds
            for p in range(2):
                for part in range(4):
                    lanes = slice(part * LANES, (part + 1) * LANES)
                    slot = block + (part // 2) * 32 + part % 2
                    out_ref[slot, p : p + 1, :] = rhs_ref[p, y, x : x + 1, lanes]
                    out_ref[slot, 2 + p : 3 + p, :] = start_ref[p, y, x : x + 1, lanes]


def pack_kernel(mat_hbm, rhs_hbm, start_hbm, out_ref, mat_ref, rhs_ref, start_ref, sems):
    copies = [
        pltpu.make_async_copy(source, target, sems.at[k])
        for k, (source, target) in enumerate(((mat_hbm, mat_ref), (rhs_hbm, rhs_ref), (start_hbm, start_ref)))
    ]
    for copy in copies:
        copy.start()
    for copy in copies:
        copy.wait()
    pack(mat_ref, rhs_ref, start_ref, out_ref)


def unpack_kernel(in_ref, forward_ref, backward_ref):
    flip_x, flip_y = flips()
    for y in range(4):
        for x in range(4):
            block = block_of(y, x, flip_y, flip_x)
            for part in range(4):
                lanes = slice(part * LANES, (part + 1) * LANES)
                slot = block + (part // 2) * 32 + part % 2
                for p in range(2):
                    forward_ref[p, y, x : x + 1, lanes] = in_ref[slot, p : p + 1, :]
                    backward_ref[p, y, x : x + 1, lanes] = in_ref[slot, 2 + p : 3 + p, :]


def masks_of(kind):
    half = (lax.broadcasted_iota(jnp.int32, kind.shape, 1) >= DOFS).astype(F32)
    mask_a = jnp.where(kind == half, 1.0, 0.0).astype(BF16)
    mask_b = jnp.where(kind == half + 2.0, 1.0, 0.0).astype(BF16)
    return mask_a, mask_b


def arrange_kernel(in_ref, rhs_ref, start_ref, kind_ref, mask_a_ref, mask_b_ref):
    for step in range(STEPS):
        for chunk in range(CHUNKS):
            block, p = chunk * (STEPS // 2) + step // 2, step % 2
            row = step * CHUNKS + chunk
            rhs_ref[row : row + 1, :] = in_ref[block, p : p + 1, :]
            start_ref[row : row + 1, :] = in_ref[block, 2 + p : 3 + p, :]
            kind_ref[row : row + 1, :] = in_ref[block, 4:5, :]
    kinds = kind_ref[...]
    low = lax.broadcasted_iota(jnp.int32, kinds.shape, 1) < DOFS
    odd = (lax.broadcasted_iota(jnp.int32, kinds.shape, 0) // CHUNKS) % 2 == 1
    kind_ref[...] = jnp.where(low == odd, pltpu.roll(kinds, DOFS, 1), kinds)
    mask_a, mask_b = masks_of(kind_ref[...])
    mask_a_ref[...] = mask_a
    mask_b_ref[...] = mask_b


def tables_kernel(diag_ref, z_ref, side_ref, tables_ref, sides_ref, own_ref, plain_ref):
    low_half = lax.broadcasted_iota(jnp.int32, (7 * DOFS, LANES), 1) < DOFS
    joined = []
    for m in range(KINDS):
        inverse = jnp.concatenate([diag_ref[m], diag_ref[m]], axis=1)
        left = jnp.concatenate([z_ref[m].reshape(2 * DOFS, DOFS), side_ref[m].reshape(4 * DOFS, DOFS)], axis=0)
        product = jnp.dot(left, inverse, precision=HIGH, preferred_element_type=F32)
        for q in range(2):
            part = product[q * DOFS : (q + 1) * DOFS]
            plain_ref[q, m] = part
            high, low = split(part)
            tables_ref[q, m * DOFS : (m + 1) * DOFS, :LANES] = high
            tables_ref[q, m * DOFS : (m + 1) * DOFS, LANES:] = low
        joined.append(jnp.concatenate([product, inverse], axis=0))
    for half in range(2):
        lanes = slice(half * LANES, (half + 1) * LANES)
        high, low = split(jnp.where(low_half, joined[2 * half], joined[2 * half + 1]))
        sides_ref[0, :, lanes] = high[2 * DOFS : 6 * DOFS]
        sides_ref[1, :, lanes] = low[2 * DOFS : 6 * DOFS]
        for k, q in enumerate((1, 6)):
            own_ref[k, :DOFS, lanes] = high[q * DOFS : (q + 1) * DOFS]
            own_ref[k, DOFS:, lanes] = low[q * DOFS : (q + 1) * DOFS]


def chain_order(descending):
    steps, chunks = list(range(STEPS)), list(range(CHUNKS))
    return (steps[::-1], chunks[::-1]) if descending else (steps, chunks)


def maps_kernel(q, kind_ref, mask_a_ref, mask_b_ref, tables_ref, plain_ref, after_ref, map_ref, run_ref, wide_ref):
    order = chain_order(q == 1)[0]
    for chunk in range(CHUNKS):
        row = order[0] * CHUNKS + chunk
        kind = jnp.broadcast_to(kind_ref[row : row + 1, :], (DOFS, LANES))
        first = jnp.where(kind == 0.0, plain_ref[q, 0], plain_ref[q, 1])
        second = jnp.where(kind == 2.0, plain_ref[q, 2], plain_ref[q, 3])
        run_ref[chunk] = jnp.where(kind < 2.0, first, second)
    for step in order[1:]:
        rows = pl.ds(step * CHUNKS, CHUNKS)
        mask_a, mask_b = mask_a_ref[rows, :], mask_b_ref[rows, :]
        for group in range(CHUNKS // 4):
            for k in range(4):
                chunk = group * 4 + k
                a = jnp.broadcast_to(mask_a[chunk : chunk + 1, :], (DOFS, LANES))
                b = jnp.broadcast_to(mask_b[chunk : chunk + 1, :], (DOFS, LANES))
                wide_ref[k * 2 * DOFS : (k + 1) * 2 * DOFS, :] = widened(run_ref[chunk], a, b)
            product = jnp.dot(wide_ref[...], tables_ref[q], preferred_element_type=F32)
            for k in range(4):
                run_ref[group * 4 + k] = fold(product[k * 2 * DOFS : (k + 1) * 2 * DOFS])
    for place, chunk in enumerate(chain_order(q == 1)[1]):
        product = run_ref[chunk]
        if place % 2 == 1:
            turned = product.T[:DOFS]
            product = jnp.concatenate([turned, turned], axis=1)
        map_ref[chunk] = product


def both(mask):
    return jnp.concatenate([mask, mask], axis=0)


def pairs_of(state):
    low = lax.broadcasted_iota(jnp.int32, (CHUNKS, LANES), 1) < DOFS
    return jnp.where(low, state[:CHUNKS], state[CHUNKS:])


def chain(const_ref, mask_a_ref, mask_b_ref, table_ref, map_ref, ends_ref, heads_ref, out_ref, descending):
    steps, chunks = chain_order(descending)

    def known(step):
        rows = pl.ds(step * CHUNKS, CHUNKS)
        return jnp.concatenate([const_ref[rows, :], const_ref[pl.ds(ROWS + step * CHUNKS, CHUNKS), :]], axis=0)

    def advance(state, step):
        rows = pl.ds(step * CHUNKS, CHUNKS)
        wide = widened(state, both(mask_a_ref[rows, :]), both(mask_b_ref[rows, :]))
        product = jnp.dot(wide, table_ref[...], preferred_element_type=F32)
        return known(step) - fold(product)

    state = known(steps[0])
    for step in steps[1:]:
        state = advance(state, step)
    ends_ref[...] = pairs_of(state)

    row = lax.broadcasted_iota(jnp.int32, (DOFS, LANES), 0)
    lane = lax.broadcasted_iota(jnp.int32, (DOFS, LANES), 1)
    low = lane < DOFS
    unit = jnp.where((lane & (DOFS - 1)) == row, 1.0, 0.0)
    upright = jnp.zeros((DOFS, LANES), F32)
    for place, chunk in enumerate(chunks):
        end = ends_ref[chunk : chunk + 1, :]
        if place % 2 == 0:
            heads_ref[chunk : chunk + 1, :] = jnp.sum(upright * unit, axis=0, keepdims=True)
            flat = jnp.sum(upright * map_ref[chunk], axis=0, keepdims=True) + end
        else:
            heads_ref[chunk : chunk + 1, :] = flat
            terms = flat * map_ref[chunk] + end * unit
            first = jnp.sum(jnp.where(low, terms, 0.0), axis=1, keepdims=True)
            second = jnp.sum(jnp.where(low, 0.0, terms), axis=1, keepdims=True)
            upright = jnp.where(low, first, second)

    state = doubled(heads_ref[...])
    for step in steps:
        state = advance(state, step)
        out_ref[pl.ds(step * CHUNKS, CHUNKS), :] = pairs_of(state)


def beside_inside(refs):
    x, y = lax.axis_index("b"), lax.axis_index("am") * 2 + lax.axis_index("al")
    x = jnp.where(lax.axis_index("gx") == 1, 7 - x, x)
    y = jnp.where(lax.axis_index("gy") == 1, 7 - y, y)
    inside = (y > 0, y < 7, x > 0, x < 7)
    return [jnp.where(here, ref[...], 0.0) for here, ref in zip(inside, refs)]


def stacked(value):
    high, low = split(value)
    return jnp.concatenate([high, low], axis=0)


def beside_each_other(first, second):
    low = lax.broadcasted_iota(jnp.int32, first.shape, 1) < DOFS
    return jnp.concatenate(
        [jnp.where(low, first, pltpu.roll(second, DOFS, 1)), jnp.where(low, pltpu.roll(first, DOFS, 1), second)], axis=0
    )


def product_of(left, pair_ref):
    total = jnp.dot(left, pair_ref[0], preferred_element_type=F32)
    return total + jnp.dot(left, pair_ref[1], preferred_element_type=F32)


def chosen(product, mask_a, mask_b):
    rows = product.shape[0] // 2
    total = product[:rows] + product[rows:]
    kept = total[:, :LANES] * mask_a + total[:, LANES:] * mask_b
    return kept + pltpu.roll(kept, DOFS, 1)


def side_product(pieces, sides_ref):
    left = jnp.concatenate([beside_each_other(*pieces[:2]), beside_each_other(*pieces[2:])], axis=1)
    return product_of(stacked(left), sides_ref)


def own_product(piece, pair_ref):
    return jnp.dot(stacked(doubled(piece)), pair_ref[...], preferred_element_type=F32)


def forward_kernel(rhs_ref, start_ref, n0_ref, n1_ref, n2_ref, n3_ref, mask_a_ref, mask_b_ref, tables_ref,
                   sides_ref, own_ref, map_ref, forward_ref, given_ref, const_ref, ends_ref, heads_ref):
    mask_a, mask_b = both(mask_a_ref[...].astype(F32)), both(mask_b_ref[...].astype(F32))
    start = start_ref[...]
    following = jnp.concatenate([start[1:CHUNKS], jnp.zeros((1, LANES), F32)], axis=0)
    upper = jnp.concatenate([start[CHUNKS:], following], axis=0)
    product = side_product(beside_inside((n0_ref, n1_ref, n2_ref, n3_ref)), sides_ref)
    given = chosen(product + own_product(upper, own_ref.at[0]), mask_a, mask_b)
    given_ref[...] = given
    const_ref[...] = chosen(own_product(rhs_ref[...], own_ref.at[1]), mask_a, mask_b) - given
    chain(const_ref, mask_a_ref, mask_b_ref, tables_ref.at[0], map_ref, ends_ref, heads_ref, forward_ref, False)


def backward_kernel(forward_ref, given_ref, n0_ref, n1_ref, n2_ref, n3_ref, mask_a_ref, mask_b_ref, tables_ref,
                    sides_ref, map_ref, out_ref, const_ref, ends_ref, heads_ref, backward_ref):
    mask_a, mask_b = both(mask_a_ref[...].astype(F32)), both(mask_b_ref[...].astype(F32))
    terms = chosen(side_product(beside_inside((n0_ref, n1_ref, n2_ref, n3_ref)), sides_ref), mask_a, mask_b)
    const_ref[...] = doubled(forward_ref[...]) + (given_ref[...] - terms)
    chain(const_ref, mask_a_ref, mask_b_ref, tables_ref.at[1], map_ref, ends_ref, heads_ref, backward_ref, True)
    for step in range(STEPS):
        for chunk in range(CHUNKS):
            block, p = chunk * (STEPS // 2) + step // 2, step % 2
            row = step * CHUNKS + chunk
            out_ref[block, p : p + 1, :] = forward_ref[row : row + 1, :]
            out_ref[block, 2 + p : 3 + p, :] = backward_ref[row : row + 1, :]


def shape(*dims, dtype=F32):
    return jax.ShapeDtypeStruct(dims, dtype)


def call(kernel, outs, ins, scratch=(), flops=1000000, limit=16 * 1024 * 1024):
    return pl.pallas_call(
        kernel,
        out_shape=outs,
        in_specs=ins,
        out_specs=jax.tree.map(lambda _: VMEM, outs),
        scratch_shapes=scratch,
        cost_estimate=pl.CostEstimate(flops=flops, bytes_accessed=500000, transcendentals=0),
        compiler_params=pltpu.CompilerParams(vmem_limit_bytes=limit),
    )


X_AXES, Y_AXES = ("b", "gx"), ("am", "al", "gy")
RING = [0, 2, 4, 6, 7, 5, 3, 1]


def moved(value, axes, distance):
    pairs = [(RING[i], RING[(i + distance) % 8]) for i in range(8)]
    return lax.ppermute(value, axes, pairs)


def neighbours(value):
    return [
        moved(value, Y_AXES, 1),
        moved(value, Y_AXES, -1),
        moved(value, X_AXES, 1),
        moved(value, X_AXES, -1),
    ]


def per_device(rhs_field, start_field, material, diag_inverse, z_blocks, side_blocks):
    mask = shape(ROWS, LANES, dtype=BF16)
    field = shape(ROWS, LANES)
    packed = call(
        pack_kernel,
        shape(PEERS, SLOTS, LANES),
        [HBM] * 3,
        [
            pltpu.SMEM(material.shape, jnp.int32),
            pltpu.VMEM(rhs_field.shape, F32),
            pltpu.VMEM(rhs_field.shape, F32),
            pltpu.SemaphoreType.DMA((3,)),
        ],
        limit=None,
    )(material, rhs_field, start_field)
    arrived = lax.all_to_all(packed, GZ, 0, 0, tiled=True)
    square = shape(2, 256, 256, dtype=BF16)
    tables, sides, own, plain = call(
        tables_kernel,
        (square, square, shape(2, 2 * DOFS, 256, dtype=BF16), shape(2, KINDS, DOFS, LANES)),
        [VMEM] * 3,
        flops=4000000000,
    )(diag_inverse, z_blocks, side_blocks)
    rhs, start, kind, mask_a, mask_b = call(arrange_kernel, (field, field, field, mask, mask), [VMEM])(arrived)
    beside = neighbours(start)

    def maps(q, after):
        return call(
            functools.partial(maps_kernel, q),
            shape(CHUNKS, DOFS, LANES),
            [VMEM] * 5 + [pl.BlockSpec(memory_space=pl.ANY)],
            [pltpu.VMEM((CHUNKS, DOFS, LANES), F32), pltpu.VMEM((8 * DOFS, 256), BF16)],
            flops=4000000000,
        )(kind, mask_a, mask_b, tables, plain, after)

    map_f = maps(0, start)
    chain_scratch = [
        pltpu.VMEM((2 * ROWS, LANES), F32),
        pltpu.VMEM((CHUNKS, LANES), F32),
        pltpu.VMEM((CHUNKS, LANES), F32),
    ]
    forward, given = call(
        forward_kernel,
        (field, shape(2 * ROWS, LANES)),
        [VMEM] * 12,
        chain_scratch,
        flops=4000000000,
    )(rhs, start, *beside, mask_a, mask_b, tables, sides, own, map_f)

    beside = neighbours(forward)
    map_b = maps(1, forward)
    ready = call(
        backward_kernel,
        shape(PEERS, 4, LANES),
        [VMEM] * 11,
        chain_scratch + [pltpu.VMEM((ROWS, LANES), F32)],
        flops=4000000000,
    )(forward, given, *beside, mask_a, mask_b, tables, sides, map_b)
    returned = lax.all_to_all(ready, GZ, 0, 0, tiled=True)
    cells = shape(*rhs_field.shape)
    return call(unpack_kernel, (cells, cells), [VMEM])(returned)


def solution(mesh):
    finer = Mesh(
        mesh.devices.reshape(2, 2, 2, 4, 2, mesh.shape["gx"], mesh.shape["gy"]),
        GZ + ("gx", "gy"),
    )
    placed = (P(GZ, "gy", "gx", None), P(GZ, "gy", "gx", None), P(GZ, "gy", "gx"), P(), P(), P())
    return jax.shard_map(
        per_device,
        mesh=finer,
        in_specs=placed,
        out_specs=(P(GZ, "gy", "gx", None), P(GZ, "gy", "gx", None)),
        check_vma=False,
    )
```

```python
import functools

import jax
import jax.numpy as jnp
from jax import lax
from jax.experimental import pallas as pl
from jax.experimental.pallas import tpu as pltpu
from jax.sharding import Mesh
from jax.sharding import PartitionSpec as P

GZ = ("ah", "am", "al", "b", "c")
HIGH = lax.Precision.HIGHEST
F32 = jnp.float32
BF16 = jnp.bfloat16

LANES = 128
DOFS = 64
KINDS = 4
STEPS = 4
CHUNKS = 128 // STEPS
ROWS = STEPS * CHUNKS
PEERS = 64
SLOTS = 5
VMEM = pl.BlockSpec(memory_space=pltpu.VMEM)
HBM = pl.BlockSpec(memory_space=pltpu.HBM)


def split(value):
    high = value.astype(BF16)
    return high, (value - high.astype(F32)).astype(BF16)


def doubled(pairs):
    low = lax.broadcasted_iota(jnp.int32, pairs.shape, 1) < DOFS
    turned = pltpu.roll(pairs, DOFS, 1)
    return jnp.concatenate([jnp.where(low, pairs, turned), jnp.where(low, turned, pairs)], axis=0)


def fold(product):
    rows = product.shape[0] // 2
    top, bottom = product[:rows], product[rows:]
    return (top[:, :LANES] + top[:, LANES:]) + (bottom[:, :LANES] + bottom[:, LANES:])


def widened(value, mask_a, mask_b):
    high, low = split(value)
    return jnp.concatenate(
        [
            jnp.concatenate([high * mask_a, high * mask_b], axis=1),
            jnp.concatenate([low * mask_a, low * mask_b], axis=1),
        ],
        axis=0,
    )


def block_of(y, x, flip_y, flip_x):
    return (y ^ flip_y) * 8 + (x ^ flip_x) * 2


def flips():
    return lax.axis_index("gx") * 3, lax.axis_index("gy") * 3


def pack_kernel(mat_hbm, rhs_hbm, start_hbm, out_hbm, mat_ref, rhs_ref, start_ref, out_ref, sems, out_sems):
    copies = [
        pltpu.make_async_copy(source, target, sems.at[k])
        for k, (source, target) in enumerate(((mat_hbm, mat_ref), (rhs_hbm, rhs_ref), (start_hbm, start_ref)))
    ]
    for copy in copies:
        copy.start()
    for copy in copies:
        copy.wait()
    flip_x, flip_y = flips()
    low = lax.broadcasted_iota(jnp.int32, (1, LANES), 1) < DOFS
    leaving = []
    for y in range(4):
        for x in range(4):
            block = block_of(y, x, flip_y, flip_x)
            kinds = jnp.where(low, mat_ref[0, y, x].astype(F32), mat_ref[1, y, x].astype(F32))
            for part in range(4):
                lanes = slice(part * LANES, (part + 1) * LANES)
                slot = block + (part // 2) * 32 + part % 2
                out_ref[slot, 4:5, :] = kinds
                for p in range(2):
                    out_ref[slot, p : p + 1, :] = rhs_ref[p, y, x : x + 1, lanes]
                    out_ref[slot, 2 + p : 3 + p, :] = start_ref[p, y, x : x + 1, lanes]
        for half in range(2):
            slots = pl.ds(half * 32 + (y ^ flip_y) * 8, 8)
            copy = pltpu.make_async_copy(out_ref.at[slots], out_hbm.at[slots], out_sems.at[y, half])
            copy.start()
            leaving.append(copy)
    for copy in leaving:
        copy.wait()


def unpack_kernel(in_ref, forward_hbm, backward_hbm, forward_ref, backward_ref, sems):
    flip_x, flip_y = flips()
    leaving = []
    for k, (field_ref, field_hbm) in enumerate(((forward_ref, forward_hbm), (backward_ref, backward_hbm))):
        for p in range(2):
            for y in range(4):
                for x in range(4):
                    block = block_of(y, x, flip_y, flip_x)
                    for part in range(4):
                        lanes = slice(part * LANES, (part + 1) * LANES)
                        slot = block + (part // 2) * 32 + part % 2
                        field_ref[p, y, x : x + 1, lanes] = in_ref[slot, 2 * k + p : 2 * k + p + 1, :]
            copy = pltpu.make_async_copy(field_ref.at[p], field_hbm.at[p], sems.at[k, p])
            copy.start()
            leaving.append(copy)
    for copy in leaving:
        copy.wait()


def masks_of(kind):
    half = (lax.broadcasted_iota(jnp.int32, kind.shape, 1) >= DOFS).astype(F32)
    mask_a = jnp.where(kind == half, 1.0, 0.0).astype(BF16)
    mask_b = jnp.where(kind == half + 2.0, 1.0, 0.0).astype(BF16)
    return mask_a, mask_b


def arrange_kernel(in_ref, rhs_ref, start_ref, kind_ref, mask_a_ref, mask_b_ref):
    for step in range(STEPS):
        for chunk in range(CHUNKS):
            block, p = chunk * (STEPS // 2) + step // 2, step % 2
            row = step * CHUNKS + chunk
            rhs_ref[row : row + 1, :] = in_ref[block, p : p + 1, :]
            start_ref[row : row + 1, :] = in_ref[block, 2 + p : 3 + p, :]
            kind_ref[row : row + 1, :] = in_ref[block, 4:5, :]
    kinds = kind_ref[...]
    low = lax.broadcasted_iota(jnp.int32, kinds.shape, 1) < DOFS
    odd = (lax.broadcasted_iota(jnp.int32, kinds.shape, 0) // CHUNKS) % 2 == 1
    kind_ref[...] = jnp.where(low == odd, pltpu.roll(kinds, DOFS, 1), kinds)
    mask_a, mask_b = masks_of(kind_ref[...])
    mask_a_ref[...] = mask_a
    mask_b_ref[...] = mask_b


def tables_kernel(diag_ref, z_ref, side_ref, tables_ref, sides_ref, own_ref, plain_ref):
    low_half = lax.broadcasted_iota(jnp.int32, (7 * DOFS, LANES), 1) < DOFS
    joined = []
    for m in range(KINDS):
        inverse = jnp.concatenate([diag_ref[m], diag_ref[m]], axis=1)
        left = jnp.concatenate([z_ref[m].reshape(2 * DOFS, DOFS), side_ref[m].reshape(4 * DOFS, DOFS)], axis=0)
        product = jnp.dot(left, inverse, precision=HIGH, preferred_element_type=F32)
        for q in range(2):
            part = product[q * DOFS : (q + 1) * DOFS]
            plain_ref[q, m] = part
            high, low = split(part)
            tables_ref[q, m * DOFS : (m + 1) * DOFS, :LANES] = high
            tables_ref[q, m * DOFS : (m + 1) * DOFS, LANES:] = low
        joined.append(jnp.concatenate([product, inverse], axis=0))
    for half in range(2):
        lanes = slice(half * LANES, (half + 1) * LANES)
        high, low = split(jnp.where(low_half, joined[2 * half], joined[2 * half + 1]))
        sides_ref[0, :, lanes] = high[2 * DOFS : 6 * DOFS]
        sides_ref[1, :, lanes] = low[2 * DOFS : 6 * DOFS]
        for k, q in enumerate((1, 6)):
            own_ref[k, :DOFS, lanes] = high[q * DOFS : (q + 1) * DOFS]
            own_ref[k, DOFS:, lanes] = low[q * DOFS : (q + 1) * DOFS]


def chain_order(descending):
    steps, chunks = list(range(STEPS)), list(range(CHUNKS))
    return (steps[::-1], chunks[::-1]) if descending else (steps, chunks)


def maps_kernel(q, kind_ref, mask_a_ref, mask_b_ref, tables_ref, plain_ref, after_ref, map_ref, run_ref, wide_ref):
    order = chain_order(q == 1)[0]
    for chunk in range(CHUNKS):
        row = order[0] * CHUNKS + chunk
        kind = jnp.broadcast_to(kind_ref[row : row + 1, :], (DOFS, LANES))
        first = jnp.where(kind == 0.0, plain_ref[q, 0], plain_ref[q, 1])
        second = jnp.where(kind == 2.0, plain_ref[q, 2], plain_ref[q, 3])
        run_ref[chunk] = jnp.where(kind < 2.0, first, second)
    for step in order[1:]:
        rows = pl.ds(step * CHUNKS, CHUNKS)
        mask_a, mask_b = mask_a_ref[rows, :], mask_b_ref[rows, :]
        for group in range(CHUNKS // 4):
            for k in range(4):
                chunk = group * 4 + k
                a = jnp.broadcast_to(mask_a[chunk : chunk + 1, :], (DOFS, LANES))
                b = jnp.broadcast_to(mask_b[chunk : chunk + 1, :], (DOFS, LANES))
                wide_ref[k * 2 * DOFS : (k + 1) * 2 * DOFS, :] = widened(run_ref[chunk], a, b)
            product = jnp.dot(wide_ref[...], tables_ref[q], preferred_element_type=F32)
            for k in range(4):
                run_ref[group * 4 + k] = fold(product[k * 2 * DOFS : (k + 1) * 2 * DOFS])
    for place, chunk in enumerate(chain_order(q == 1)[1]):
        product = run_ref[chunk]
        if place % 2 == 1:
            turned = product.T[:DOFS]
            product = jnp.concatenate([turned, turned], axis=1)
        map_ref[chunk] = product


def both(mask):
    return jnp.concatenate([mask, mask], axis=0)


def pairs_of(state):
    low = lax.broadcasted_iota(jnp.int32, (CHUNKS, LANES), 1) < DOFS
    return jnp.where(low, state[:CHUNKS], state[CHUNKS:])


def rows_of(step):
    return pl.ds(step * CHUNKS, CHUNKS)


def chain(known, mask_a_ref, mask_b_ref, table_ref, map_ref, ends_ref, heads_ref, out_ref, descending):
    steps, chunks = chain_order(descending)
    consts = {}

    def advance(state, step):
        rows = rows_of(step)
        wide = widened(state, both(mask_a_ref[rows, :]), both(mask_b_ref[rows, :]))
        product = jnp.dot(wide, table_ref[...], preferred_element_type=F32)
        return consts[step] - fold(product)

    state = consts[steps[0]] = known(steps[0])
    for step in steps[1:]:
        consts[step] = known(step)
        state = advance(state, step)
    ends_ref[...] = pairs_of(state)

    row = lax.broadcasted_iota(jnp.int32, (DOFS, LANES), 0)
    lane = lax.broadcasted_iota(jnp.int32, (DOFS, LANES), 1)
    low = lane < DOFS
    unit = jnp.where((lane & (DOFS - 1)) == row, 1.0, 0.0)
    upright = jnp.zeros((DOFS, LANES), F32)
    for place, chunk in enumerate(chunks):
        end = ends_ref[chunk : chunk + 1, :]
        if place % 2 == 0:
            heads_ref[chunk : chunk + 1, :] = jnp.sum(upright * unit, axis=0, keepdims=True)
            flat = jnp.sum(upright * map_ref[chunk], axis=0, keepdims=True) + end
        else:
            heads_ref[chunk : chunk + 1, :] = flat
            terms = flat * map_ref[chunk] + end * unit
            first = jnp.sum(jnp.where(low, terms, 0.0), axis=1, keepdims=True)
            second = jnp.sum(jnp.where(low, 0.0, terms), axis=1, keepdims=True)
            upright = jnp.where(low, first, second)

    state = doubled(heads_ref[...])
    for step in steps:
        state = advance(state, step)
        out_ref[pl.ds(step * CHUNKS, CHUNKS), :] = pairs_of(state)


def inside():
    x, y = lax.axis_index("b"), lax.axis_index("am") * 2 + lax.axis_index("al")
    x = jnp.where(lax.axis_index("gx") == 1, 7 - x, x)
    y = jnp.where(lax.axis_index("gy") == 1, 7 - y, y)
    return y > 0, y < 7, x > 0, x < 7


def stacked(value):
    high, low = split(value)
    return jnp.concatenate([high, low], axis=0)


def beside_each_other(first, second):
    low = lax.broadcasted_iota(jnp.int32, first.shape, 1) < DOFS
    return jnp.concatenate(
        [jnp.where(low, first, pltpu.roll(second, DOFS, 1)), jnp.where(low, pltpu.roll(first, DOFS, 1), second)], axis=0
    )


def product_of(left, pair_ref):
    total = jnp.dot(left, pair_ref[0], preferred_element_type=F32)
    return total + jnp.dot(left, pair_ref[1], preferred_element_type=F32)


def chosen(product, mask_a, mask_b):
    rows = product.shape[0] // 2
    total = product[:rows] + product[rows:]
    kept = total[:, :LANES] * mask_a + total[:, LANES:] * mask_b
    return kept + pltpu.roll(kept, DOFS, 1)


def side_product(pieces, sides_ref):
    left = jnp.concatenate([beside_each_other(*pieces[:2]), beside_each_other(*pieces[2:])], axis=1)
    return product_of(stacked(left), sides_ref)


def own_product(piece, pair_ref):
    return jnp.dot(stacked(doubled(piece)), pair_ref[...], preferred_element_type=F32)


def side_known(step, here, refs, sides_ref):
    rows = rows_of(step)
    return side_product([jnp.where(ok, ref[rows, :], 0.0) for ok, ref in zip(here, refs)], sides_ref)


def forward_kernel(rhs_ref, start_ref, n0_ref, n1_ref, n2_ref, n3_ref, mask_a_ref, mask_b_ref, tables_ref,
                   sides_ref, own_ref, map_ref, forward_ref, given_ref, ends_ref, heads_ref):
    here = inside()

    def known(step):
        rows = rows_of(step)
        if step + 1 < STEPS:
            upper = start_ref[rows_of(step + 1), :]
        else:
            upper = jnp.concatenate([start_ref[1:CHUNKS, :], jnp.zeros((1, LANES), F32)], axis=0)
        mask_a, mask_b = both(mask_a_ref[rows, :].astype(F32)), both(mask_b_ref[rows, :].astype(F32))
        product = side_known(step, here, (n0_ref, n1_ref, n2_ref, n3_ref), sides_ref)
        given = chosen(product + own_product(upper, own_ref.at[0]), mask_a, mask_b)
        given_ref[step] = given
        return chosen(own_product(rhs_ref[rows, :], own_ref.at[1]), mask_a, mask_b) - given

    chain(known, mask_a_ref, mask_b_ref, tables_ref.at[0], map_ref, ends_ref, heads_ref, forward_ref, False)


def backward_kernel(forward_ref, given_ref, n0_ref, n1_ref, n2_ref, n3_ref, mask_a_ref, mask_b_ref, tables_ref,
                    sides_ref, map_ref, out_ref, ends_ref, heads_ref, backward_ref):
    here = inside()

    def known(step):
        rows = rows_of(step)
        mask_a, mask_b = both(mask_a_ref[rows, :].astype(F32)), both(mask_b_ref[rows, :].astype(F32))
        terms = chosen(side_known(step, here, (n0_ref, n1_ref, n2_ref, n3_ref), sides_ref), mask_a, mask_b)
        return doubled(forward_ref[rows, :]) + (given_ref[step] - terms)

    chain(known, mask_a_ref, mask_b_ref, tables_ref.at[1], map_ref, ends_ref, heads_ref, backward_ref, True)
    for step in range(STEPS):
        for chunk in range(CHUNKS):
            block, p = chunk * (STEPS // 2) + step // 2, step % 2
            row = step * CHUNKS + chunk
            out_ref[block, p : p + 1, :] = forward_ref[row : row + 1, :]
            out_ref[block, 2 + p : 3 + p, :] = backward_ref[row : row + 1, :]


def shape(*dims, dtype=F32):
    return jax.ShapeDtypeStruct(dims, dtype)


def call(kernel, outs, ins, scratch=(), flops=1000000, limit=16 * 1024 * 1024, to=VMEM):
    return pl.pallas_call(
        kernel,
        out_shape=outs,
        in_specs=ins,
        out_specs=jax.tree.map(lambda _: to, outs),
        scratch_shapes=scratch,
        cost_estimate=pl.CostEstimate(flops=flops, bytes_accessed=500000, transcendentals=0),
        compiler_params=pltpu.CompilerParams(vmem_limit_bytes=limit),
    )


X_AXES, Y_AXES = ("b", "gx"), ("am", "al", "gy")
RING = [0, 2, 4, 6, 7, 5, 3, 1]


def moved(value, axes, distance):
    pairs = [(RING[i], RING[(i + distance) % 8]) for i in range(8)]
    return lax.ppermute(value, axes, pairs)


def neighbours(value):
    return [
        moved(value, Y_AXES, 1),
        moved(value, Y_AXES, -1),
        moved(value, X_AXES, 1),
        moved(value, X_AXES, -1),
    ]


def per_device(rhs_field, start_field, material, diag_inverse, z_blocks, side_blocks):
    mask = shape(ROWS, LANES, dtype=BF16)
    field = shape(ROWS, LANES)
    packed = call(
        pack_kernel,
        shape(PEERS, SLOTS, LANES),
        [HBM] * 3,
        [
            pltpu.SMEM(material.shape, jnp.int32),
            pltpu.VMEM(rhs_field.shape, F32),
            pltpu.VMEM(rhs_field.shape, F32),
            pltpu.VMEM((PEERS, SLOTS, LANES), F32),
            pltpu.SemaphoreType.DMA((3,)),
            pltpu.SemaphoreType.DMA((4, 2)),
        ],
        limit=None,
        to=HBM,
    )(material, rhs_field, start_field)
    arrived = lax.all_to_all(packed, GZ, 0, 0, tiled=True)
    square = shape(2, 256, 256, dtype=BF16)
    tables, sides, own, plain = call(
        tables_kernel,
        (square, square, shape(2, 2 * DOFS, 256, dtype=BF16), shape(2, KINDS, DOFS, LANES)),
        [VMEM] * 3,
        flops=4000000000,
    )(diag_inverse, z_blocks, side_blocks)
    rhs, start, kind, mask_a, mask_b = call(arrange_kernel, (field, field, field, mask, mask), [VMEM])(arrived)
    beside = neighbours(start)

    def maps(q, after):
        return call(
            functools.partial(maps_kernel, q),
            shape(CHUNKS, DOFS, LANES),
            [VMEM] * 5 + [pl.BlockSpec(memory_space=pl.ANY)],
            [pltpu.VMEM((CHUNKS, DOFS, LANES), F32), pltpu.VMEM((8 * DOFS, 256), BF16)],
            flops=4000000000,
        )(kind, mask_a, mask_b, tables, plain, after)

    map_f = maps(0, start)
    chain_scratch = [
        pltpu.VMEM((CHUNKS, LANES), F32),
        pltpu.VMEM((CHUNKS, LANES), F32),
    ]
    forward, given = call(
        forward_kernel,
        (field, shape(STEPS, 2 * CHUNKS, LANES)),
        [VMEM] * 12,
        chain_scratch,
        flops=4000000000,
    )(rhs, start, *beside, mask_a, mask_b, tables, sides, own, map_f)

    beside = neighbours(forward)
    map_b = maps(1, forward)
    ready = call(
        backward_kernel,
        shape(PEERS, 4, LANES),
        [VMEM] * 11,
        chain_scratch + [pltpu.VMEM((ROWS, LANES), F32)],
        flops=4000000000,
    )(forward, given, *beside, mask_a, mask_b, tables, sides, map_b)
    returned = lax.all_to_all(ready, GZ, 0, 0, tiled=True)
    cells = shape(*rhs_field.shape)
    return call(
        unpack_kernel,
        (cells, cells),
        [VMEM],
        [
            pltpu.VMEM(rhs_field.shape, F32),
            pltpu.VMEM(rhs_field.shape, F32),
            pltpu.SemaphoreType.DMA((2, 2)),
        ],
        to=HBM,
    )(returned)


def solution(mesh):
    finer = Mesh(
        mesh.devices.reshape(2, 2, 2, 4, 2, mesh.shape["gx"], mesh.shape["gy"]),
        GZ + ("gx", "gy"),
    )
    placed = (P(GZ, "gy", "gx", None), P(GZ, "gy", "gx", None), P(GZ, "gy", "gx"), P(), P(), P())
    return jax.shard_map(
        per_device,
        mesh=finer,
        in_specs=placed,
        out_specs=(P(GZ, "gy", "gx", None), P(GZ, "gy", "gx", None)),
        check_vma=False,
    )
```

```python
import functools

import jax
import jax.numpy as jnp
from jax import lax
from jax.experimental import pallas as pl
from jax.experimental.pallas import tpu as pltpu
from jax.sharding import Mesh
from jax.sharding import PartitionSpec as P

GZ = ("ah", "am", "al", "b", "c")
HIGH = lax.Precision.HIGHEST
F32 = jnp.float32
BF16 = jnp.bfloat16

LANES = 128
DOFS = 64
KINDS = 4
STEPS = 4
CHUNKS = 128 // STEPS
ROWS = STEPS * CHUNKS
PEERS = 64
SLOTS = 5
VMEM = pl.BlockSpec(memory_space=pltpu.VMEM)
HBM = pl.BlockSpec(memory_space=pltpu.HBM)


def split(value):
    high = value.astype(BF16)
    return high, (value - high.astype(F32)).astype(BF16)


def doubled(pairs):
    low = lax.broadcasted_iota(jnp.int32, pairs.shape, 1) < DOFS
    turned = pltpu.roll(pairs, DOFS, 1)
    return jnp.concatenate([jnp.where(low, pairs, turned), jnp.where(low, turned, pairs)], axis=0)


def fold(product):
    rows = product.shape[0] // 2
    top, bottom = product[:rows], product[rows:]
    return (top[:, :LANES] + top[:, LANES:]) + (bottom[:, :LANES] + bottom[:, LANES:])


def widened(value, mask_a, mask_b):
    high, low = split(value)
    return jnp.concatenate(
        [
            jnp.concatenate([high * mask_a, high * mask_b], axis=1),
            jnp.concatenate([low * mask_a, low * mask_b], axis=1),
        ],
        axis=0,
    )


def block_of(y, x, flip_y, flip_x):
    return (y ^ flip_y) * 8 + (x ^ flip_x) * 2


def flips():
    return lax.axis_index("gx") * 3, lax.axis_index("gy") * 3


def pack_kernel(mat_hbm, rhs_hbm, start_hbm, out_hbm, mat_ref, rhs_ref, start_ref, out_ref, sems, out_sems):
    copies = [
        pltpu.make_async_copy(source, target, sems.at[k])
        for k, (source, target) in enumerate(((mat_hbm, mat_ref), (rhs_hbm, rhs_ref), (start_hbm, start_ref)))
    ]
    for copy in copies:
        copy.start()
    for copy in copies:
        copy.wait()
    flip_x, flip_y = flips()
    low = lax.broadcasted_iota(jnp.int32, (1, LANES), 1) < DOFS
    leaving = []
    for y in range(4):
        for x in range(4):
            block = block_of(y, x, flip_y, flip_x)
            kinds = jnp.where(low, mat_ref[0, y, x].astype(F32), mat_ref[1, y, x].astype(F32))
            for part in range(4):
                lanes = slice(part * LANES, (part + 1) * LANES)
                slot = block + (part // 2) * 32 + part % 2
                out_ref[slot, 4:5, :] = kinds
                for p in range(2):
                    out_ref[slot, p : p + 1, :] = rhs_ref[p, y, x : x + 1, lanes]
                    out_ref[slot, 2 + p : 3 + p, :] = start_ref[p, y, x : x + 1, lanes]
        for half in range(2):
            slots = pl.ds(half * 32 + (y ^ flip_y) * 8, 8)
            copy = pltpu.make_async_copy(out_ref.at[slots], out_hbm.at[slots], out_sems.at[y, half])
            copy.start()
            leaving.append(copy)
    for copy in leaving:
        copy.wait()


def unpack_kernel(in_ref, forward_hbm, backward_hbm, forward_ref, backward_ref, sems):
    flip_x, flip_y = flips()
    leaving = []
    for k, (field_ref, field_hbm) in enumerate(((forward_ref, forward_hbm), (backward_ref, backward_hbm))):
        for p in range(2):
            for y in range(4):
                for x in range(4):
                    block = block_of(y, x, flip_y, flip_x)
                    for part in range(4):
                        lanes = slice(part * LANES, (part + 1) * LANES)
                        slot = block + (part // 2) * 32 + part % 2
                        field_ref[p, y, x : x + 1, lanes] = in_ref[slot, 2 * k + p : 2 * k + p + 1, :]
            copy = pltpu.make_async_copy(field_ref.at[p], field_hbm.at[p], sems.at[k, p])
            copy.start()
            leaving.append(copy)
    for copy in leaving:
        copy.wait()


def masks_of(kind):
    half = (lax.broadcasted_iota(jnp.int32, kind.shape, 1) >= DOFS).astype(F32)
    mask_a = jnp.where(kind == half, 1.0, 0.0).astype(BF16)
    mask_b = jnp.where(kind == half + 2.0, 1.0, 0.0).astype(BF16)
    return mask_a, mask_b


def arrange_kernel(in_ref, rhs_ref, start_ref, kind_ref, mask_a_ref, mask_b_ref):
    for step in range(STEPS):
        for chunk in range(CHUNKS):
            block, p = chunk * (STEPS // 2) + step // 2, step % 2
            row = step * CHUNKS + chunk
            rhs_ref[row : row + 1, :] = in_ref[block, p : p + 1, :]
            start_ref[row : row + 1, :] = in_ref[block, 2 + p : 3 + p, :]
            kind_ref[row : row + 1, :] = in_ref[block, 4:5, :]
    kinds = kind_ref[...]
    low = lax.broadcasted_iota(jnp.int32, kinds.shape, 1) < DOFS
    odd = (lax.broadcasted_iota(jnp.int32, kinds.shape, 0) // CHUNKS) % 2 == 1
    kind_ref[...] = jnp.where(low == odd, pltpu.roll(kinds, DOFS, 1), kinds)
    mask_a, mask_b = masks_of(kind_ref[...])
    mask_a_ref[...] = mask_a
    mask_b_ref[...] = mask_b


def tables_kernel(diag_ref, z_ref, side_ref, tables_ref, sides_ref, own_ref, plain_ref):
    low_half = lax.broadcasted_iota(jnp.int32, (7 * DOFS, LANES), 1) < DOFS
    joined = []
    for m in range(KINDS):
        inverse = jnp.concatenate([diag_ref[m], diag_ref[m]], axis=1)
        left = jnp.concatenate([z_ref[m].reshape(2 * DOFS, DOFS), side_ref[m].reshape(4 * DOFS, DOFS)], axis=0)
        product = jnp.dot(left, inverse, precision=HIGH, preferred_element_type=F32)
        for q in range(2):
            part = product[q * DOFS : (q + 1) * DOFS]
            plain_ref[q, m] = part
            high, low = split(part)
            tables_ref[q, m * DOFS : (m + 1) * DOFS, :LANES] = high
            tables_ref[q, m * DOFS : (m + 1) * DOFS, LANES:] = low
        joined.append(jnp.concatenate([product, inverse], axis=0))
    for half in range(2):
        lanes = slice(half * LANES, (half + 1) * LANES)
        high, low = split(jnp.where(low_half, joined[2 * half], joined[2 * half + 1]))
        sides_ref[0, :, lanes] = high[2 * DOFS : 6 * DOFS]
        sides_ref[1, :, lanes] = low[2 * DOFS : 6 * DOFS]
        for k, q in enumerate((1, 6)):
            own_ref[k, :DOFS, lanes] = high[q * DOFS : (q + 1) * DOFS]
            own_ref[k, DOFS:, lanes] = low[q * DOFS : (q + 1) * DOFS]


def chain_order(descending):
    steps, chunks = list(range(STEPS)), list(range(CHUNKS))
    return (steps[::-1], chunks[::-1]) if descending else (steps, chunks)


def maps_kernel(q, kind_ref, mask_a_ref, mask_b_ref, tables_ref, plain_ref, after_ref, map_ref, run_ref, wide_ref):
    order = chain_order(q == 1)[0]
    for chunk in range(CHUNKS):
        row = order[0] * CHUNKS + chunk
        kind = jnp.broadcast_to(kind_ref[row : row + 1, :], (DOFS, LANES))
        first = jnp.where(kind == 0.0, plain_ref[q, 0], plain_ref[q, 1])
        second = jnp.where(kind == 2.0, plain_ref[q, 2], plain_ref[q, 3])
        run_ref[chunk] = jnp.where(kind < 2.0, first, second)
    for step in order[1:]:
        rows = pl.ds(step * CHUNKS, CHUNKS)
        mask_a, mask_b = mask_a_ref[rows, :], mask_b_ref[rows, :]
        for group in range(CHUNKS // 4):
            for k in range(4):
                chunk = group * 4 + k
                a = jnp.broadcast_to(mask_a[chunk : chunk + 1, :], (DOFS, LANES))
                b = jnp.broadcast_to(mask_b[chunk : chunk + 1, :], (DOFS, LANES))
                wide_ref[k * 2 * DOFS : (k + 1) * 2 * DOFS, :] = widened(run_ref[chunk], a, b)
            product = jnp.dot(wide_ref[...], tables_ref[q], preferred_element_type=F32)
            for k in range(4):
                run_ref[group * 4 + k] = fold(product[k * 2 * DOFS : (k + 1) * 2 * DOFS])
    for place, chunk in enumerate(chain_order(q == 1)[1]):
        product = run_ref[chunk]
        if place % 2 == 1:
            turned = product.T[:DOFS]
            product = jnp.concatenate([turned, turned], axis=1)
        map_ref[chunk] = product


def both(mask):
    return jnp.concatenate([mask, mask], axis=0)


def pairs_of(state):
    low = lax.broadcasted_iota(jnp.int32, (CHUNKS, LANES), 1) < DOFS
    return jnp.where(low, state[:CHUNKS], state[CHUNKS:])


def rows_of(step):
    return pl.ds(step * CHUNKS, CHUNKS)


def chain(known, mask_a_ref, mask_b_ref, table_ref, map_ref, ends_ref, heads_ref, out_ref, descending):
    steps, chunks = chain_order(descending)
    consts = {}

    def advance(state, step):
        rows = rows_of(step)
        wide = widened(state, both(mask_a_ref[rows, :]), both(mask_b_ref[rows, :]))
        product = jnp.dot(wide, table_ref[...], preferred_element_type=F32)
        return consts[step] - fold(product)

    state = consts[steps[0]] = known(steps[0])
    for step in steps[1:]:
        consts[step] = known(step)
        state = advance(state, step)
    ends_ref[...] = pairs_of(state)

    row = lax.broadcasted_iota(jnp.int32, (DOFS, LANES), 0)
    lane = lax.broadcasted_iota(jnp.int32, (DOFS, LANES), 1)
    low = lane < DOFS
    unit = jnp.where((lane & (DOFS - 1)) == row, 1.0, 0.0)
    tiles = (DOFS // 8, 8, LANES)
    upright = jnp.zeros((DOFS, LANES), F32)
    standing = {}
    for place, chunk in enumerate(chunks):
        end = ends_ref[chunk : chunk + 1, :]
        if place % 2 == 0:
            standing[chunk] = jnp.sum((upright * unit).reshape(tiles), axis=0)
            flat = jnp.sum((upright * map_ref[chunk]).reshape(tiles), axis=0)
            for distance in (4, 2, 1):
                flat = flat + pltpu.roll(flat, distance, 0)
            flat = flat + end
        else:
            heads_ref[chunk : chunk + 1, :] = flat[0:1]
            terms = (flat[None] * map_ref[chunk].reshape(tiles)).reshape(DOFS, LANES) + end * unit
            first = jnp.sum(jnp.where(low, terms, 0.0), axis=1, keepdims=True)
            second = jnp.sum(jnp.where(low, 0.0, terms), axis=1, keepdims=True)
            upright = jnp.where(low, first, second)
    for chunk, parts in standing.items():
        heads_ref[chunk : chunk + 1, :] = jnp.sum(parts, axis=0, keepdims=True)

    state = doubled(heads_ref[...])
    for step in steps:
        state = advance(state, step)
        out_ref[pl.ds(step * CHUNKS, CHUNKS), :] = pairs_of(state)


def inside():
    x, y = lax.axis_index("b"), lax.axis_index("am") * 2 + lax.axis_index("al")
    x = jnp.where(lax.axis_index("gx") == 1, 7 - x, x)
    y = jnp.where(lax.axis_index("gy") == 1, 7 - y, y)
    return y > 0, y < 7, x > 0, x < 7


def stacked(value):
    high, low = split(value)
    return jnp.concatenate([high, low], axis=0)


def beside_each_other(first, second):
    low = lax.broadcasted_iota(jnp.int32, first.shape, 1) < DOFS
    return jnp.concatenate(
        [jnp.where(low, first, pltpu.roll(second, DOFS, 1)), jnp.where(low, pltpu.roll(first, DOFS, 1), second)], axis=0
    )


def product_of(left, pair_ref):
    total = jnp.dot(left, pair_ref[0], preferred_element_type=F32)
    return total + jnp.dot(left, pair_ref[1], preferred_element_type=F32)


def chosen(product, mask_a, mask_b):
    rows = product.shape[0] // 2
    total = product[:rows] + product[rows:]
    kept = total[:, :LANES] * mask_a + total[:, LANES:] * mask_b
    return kept + pltpu.roll(kept, DOFS, 1)


def side_product(pieces, sides_ref):
    left = jnp.concatenate([beside_each_other(*pieces[:2]), beside_each_other(*pieces[2:])], axis=1)
    return product_of(stacked(left), sides_ref)


def own_product(piece, pair_ref):
    return jnp.dot(stacked(doubled(piece)), pair_ref[...], preferred_element_type=F32)


def side_known(step, here, refs, sides_ref):
    rows = rows_of(step)
    return side_product([jnp.where(ok, ref[rows, :], 0.0) for ok, ref in zip(here, refs)], sides_ref)


def forward_kernel(rhs_ref, start_ref, n0_ref, n1_ref, n2_ref, n3_ref, mask_a_ref, mask_b_ref, tables_ref,
                   sides_ref, own_ref, map_ref, forward_ref, given_ref, ends_ref, heads_ref):
    here = inside()

    def known(step):
        rows = rows_of(step)
        if step + 1 < STEPS:
            upper = start_ref[rows_of(step + 1), :]
        else:
            upper = jnp.concatenate([start_ref[1:CHUNKS, :], jnp.zeros((1, LANES), F32)], axis=0)
        mask_a, mask_b = both(mask_a_ref[rows, :].astype(F32)), both(mask_b_ref[rows, :].astype(F32))
        product = side_known(step, here, (n0_ref, n1_ref, n2_ref, n3_ref), sides_ref)
        given = chosen(product + own_product(upper, own_ref.at[0]), mask_a, mask_b)
        given_ref[step] = given
        return chosen(own_product(rhs_ref[rows, :], own_ref.at[1]), mask_a, mask_b) - given

    chain(known, mask_a_ref, mask_b_ref, tables_ref.at[0], map_ref, ends_ref, heads_ref, forward_ref, False)


def backward_kernel(forward_ref, given_ref, n0_ref, n1_ref, n2_ref, n3_ref, mask_a_ref, mask_b_ref, tables_ref,
                    sides_ref, map_ref, out_ref, ends_ref, heads_ref, backward_ref):
    here = inside()

    def known(step):
        rows = rows_of(step)
        mask_a, mask_b = both(mask_a_ref[rows, :].astype(F32)), both(mask_b_ref[rows, :].astype(F32))
        terms = chosen(side_known(step, here, (n0_ref, n1_ref, n2_ref, n3_ref), sides_ref), mask_a, mask_b)
        return doubled(forward_ref[rows, :]) + (given_ref[step] - terms)

    chain(known, mask_a_ref, mask_b_ref, tables_ref.at[1], map_ref, ends_ref, heads_ref, backward_ref, True)
    for step in range(STEPS):
        for chunk in range(CHUNKS):
            block, p = chunk * (STEPS // 2) + step // 2, step % 2
            row = step * CHUNKS + chunk
            out_ref[block, p : p + 1, :] = forward_ref[row : row + 1, :]
            out_ref[block, 2 + p : 3 + p, :] = backward_ref[row : row + 1, :]


def shape(*dims, dtype=F32):
    return jax.ShapeDtypeStruct(dims, dtype)


def call(kernel, outs, ins, scratch=(), flops=1000000, limit=16 * 1024 * 1024, to=VMEM):
    return pl.pallas_call(
        kernel,
        out_shape=outs,
        in_specs=ins,
        out_specs=jax.tree.map(lambda _: to, outs),
        scratch_shapes=scratch,
        cost_estimate=pl.CostEstimate(flops=flops, bytes_accessed=500000, transcendentals=0),
        compiler_params=pltpu.CompilerParams(vmem_limit_bytes=limit),
    )


X_AXES, Y_AXES = ("b", "gx"), ("am", "al", "gy")
RING = [0, 2, 4, 6, 7, 5, 3, 1]


def moved(value, axes, distance):
    pairs = [(RING[i], RING[(i + distance) % 8]) for i in range(8)]
    return lax.ppermute(value, axes, pairs)


def neighbours(value):
    return [
        moved(value, Y_AXES, 1),
        moved(value, Y_AXES, -1),
        moved(value, X_AXES, 1),
        moved(value, X_AXES, -1),
    ]


def per_device(rhs_field, start_field, material, diag_inverse, z_blocks, side_blocks):
    mask = shape(ROWS, LANES, dtype=BF16)
    field = shape(ROWS, LANES)
    packed = call(
        pack_kernel,
        shape(PEERS, SLOTS, LANES),
        [HBM] * 3,
        [
            pltpu.SMEM(material.shape, jnp.int32),
            pltpu.VMEM(rhs_field.shape, F32),
            pltpu.VMEM(rhs_field.shape, F32),
            pltpu.VMEM((PEERS, SLOTS, LANES), F32),
            pltpu.SemaphoreType.DMA((3,)),
            pltpu.SemaphoreType.DMA((4, 2)),
        ],
        limit=None,
        to=HBM,
    )(material, rhs_field, start_field)
    arrived = lax.all_to_all(packed, GZ, 0, 0, tiled=True)
    square = shape(2, 256, 256, dtype=BF16)
    tables, sides, own, plain = call(
        tables_kernel,
        (square, square, shape(2, 2 * DOFS, 256, dtype=BF16), shape(2, KINDS, DOFS, LANES)),
        [VMEM] * 3,
        flops=4000000000,
    )(diag_inverse, z_blocks, side_blocks)
    rhs, start, kind, mask_a, mask_b = call(arrange_kernel, (field, field, field, mask, mask), [VMEM])(arrived)
    beside = neighbours(start)

    def maps(q, after):
        return call(
            functools.partial(maps_kernel, q),
            shape(CHUNKS, DOFS, LANES),
            [VMEM] * 5 + [pl.BlockSpec(memory_space=pl.ANY)],
            [pltpu.VMEM((CHUNKS, DOFS, LANES), F32), pltpu.VMEM((8 * DOFS, 256), BF16)],
            flops=4000000000,
        )(kind, mask_a, mask_b, tables, plain, after)

    map_f = maps(0, start)
    chain_scratch = [
        pltpu.VMEM((CHUNKS, LANES), F32),
        pltpu.VMEM((CHUNKS, LANES), F32),
    ]
    forward, given = call(
        forward_kernel,
        (field, shape(STEPS, 2 * CHUNKS, LANES)),
        [VMEM] * 12,
        chain_scratch,
        flops=4000000000,
    )(rhs, start, *beside, mask_a, mask_b, tables, sides, own, map_f)

    beside = neighbours(forward)
    map_b = maps(1, forward)
    ready = call(
        backward_kernel,
        shape(PEERS, 4, LANES),
        [VMEM] * 11,
        chain_scratch + [pltpu.VMEM((ROWS, LANES), F32)],
        flops=4000000000,
    )(forward, given, *beside, mask_a, mask_b, tables, sides, map_b)
    returned = lax.all_to_all(ready, GZ, 0, 0, tiled=True)
    cells = shape(*rhs_field.shape)
    return call(
        unpack_kernel,
        (cells, cells),
        [VMEM],
        [
            pltpu.VMEM(rhs_field.shape, F32),
            pltpu.VMEM(rhs_field.shape, F32),
            pltpu.SemaphoreType.DMA((2, 2)),
        ],
        to=HBM,
    )(returned)


def solution(mesh):
    finer = Mesh(
        mesh.devices.reshape(2, 2, 2, 4, 2, mesh.shape["gx"], mesh.shape["gy"]),
        GZ + ("gx", "gy"),
    )
    placed = (P(GZ, "gy", "gx", None), P(GZ, "gy", "gx", None), P(GZ, "gy", "gx"), P(), P(), P())
    return jax.shard_map(
        per_device,
        mesh=finer,
        in_specs=placed,
        out_specs=(P(GZ, "gy", "gx", None), P(GZ, "gy", "gx", None)),
        check_vma=False,
    )
```
